32 devices in a mesh: segment: 4 (over y, x), ctx: 8 (over z, core).
Axes of the slice: x: 2, y: 2, z: 4, core: 2. Of those that a mesh axis runs over, the one named last changes fastest.
Arguments:
- segment_input: bfloat16 [4, 1024, 2048], P('segment', 'ctx'), may hold values from -6 to 6
- views: bfloat16 [4, 16, 128, 384], P('segment'), may hold values from -0.5 to 0.5
- gate_vec: float32 [4, 16, 128], P('segment'), may hold values from -0.9 to 0.9
- base_rate: float32 [4, 16], P('segment'), may hold values from 0.05 to 1.5
- norm_gain: float32 [4, 16, 128], P('segment'), may hold values from 0.5 to 1.5
- init_weight: float32 [4, 16, 128, 128], P('segment'), may hold values from -0.5 to 0.5
- out_grad: bfloat16 [4, 1024, 2048], P('segment', 'ctx'), may hold values from -6 to 6
Outputs:
- next_input: bfloat16 [4, 1024, 2048], P('segment', 'ctx')
- view_grad: float32 [4, 16, 128, 384], P('segment', 'ctx')
- gate_grad: float32 [4, 16, 128], P('segment', 'ctx')
- rate_grad: float32 [4, 16], P('segment', 'ctx')
- gain_grad: float32 [4, 16, 128], P('segment', 'ctx')
- init_grad: float32 [4, 16, 128, 128], P('segment', 'ctx')
- input_grad: bfloat16 [4, 1024, 2048], P('segment', 'ctx')
The draws below stay inside these ranges and needn't reach their ends.
All inputs are finite; a program needn't handle non-finite values.
Results may differ from the reference program's by a relative error of at most 0.001.
Values may be sent and summed in bfloat16 or wider, within the bound.
A program may use at most 128 MiB of HBM per device.

```python
import math
import jax
import jax.numpy as jnp
from jax import lax

H = 16
HD = 128
MB = 16
TOKENS = 1024
SEGMENTS = 4


def steps_of(key, dims, shards, smallest, largest):
    def one(position, blocks):
        draws = jax.random.uniform(jax.random.fold_in(jax.random.fold_in(key, 6), position), (blocks,), jnp.float32, smallest / len(shards), largest / len(shards))
        return jnp.repeat(jnp.exp(draws), dims[position] // blocks).reshape((-1,) + (1,) * (len(dims) - position - 1))

    gain = one(*shards[0])
    for cut in shards[1:]:
        gain = gain * one(*cut)
    return gain


def noise(stream_key, shape, width, most, split=(), kind=jnp.bfloat16):
    values = jax.random.normal(stream_key, shape, jnp.float32) * width
    if len(split) > 0:
        values = steps_of(stream_key, shape, split, -0.22, 0.18) * values
    return jnp.clip(values, min=-most, max=most).astype(kind)


def setup_inputs(seed: int = 0) -> dict:
    key_list = jax.random.split(jax.random.key(seed), 8)
    segment_input = noise(key_list[0], (SEGMENTS, TOKENS, H * HD), 1.0, 6.0, ((0, 4), (1, 8)))
    views = noise(key_list[1], (SEGMENTS, H, HD, 3 * HD), HD ** -0.5, 0.5, ((0, 4),))
    gate_vec = noise(key_list[2], (SEGMENTS, H, HD), 0.15, 0.9, ((0, 4),), jnp.float32)
    base_rate = jnp.clip(jnp.exp(math.log(1.5) - 3.4011974 * jax.random.uniform(key_list[3], (SEGMENTS, H), jnp.float32) ** steps_of(key_list[3], (SEGMENTS, H), ((0, 4),), -0.2, 0.2)), 0.05, 1.5)
    norm_gain = jnp.clip(1.0 + 0.1 * jax.random.normal(key_list[4], (SEGMENTS, H, HD), jnp.float32), 0.5, 1.5)
    init_weight = noise(key_list[5], (SEGMENTS, H, HD, HD), HD ** -0.5, 0.5, ((0, 4),), jnp.float32)
    out_grad = noise(key_list[6], (SEGMENTS, TOKENS, H * HD), 1.0, 6.0, ((0, 4), (1, 8)))
    return dict(segment_input=segment_input, views=views, gate_vec=gate_vec, base_rate=base_rate, norm_gain=norm_gain, init_weight=init_weight, out_grad=out_grad)


HIGH = lax.Precision.HIGHEST

def head_views(view_f, gate_f, rate_f, tokens_f):
    tok_count = tokens_f.shape[0]
    head_count, head_width = gate_f.shape
    pieces = tokens_f.reshape(tok_count, head_count, head_width)
    packed = jnp.einsum('thd,hde->hte', pieces, view_f, precision=HIGH)
    queries = packed[:, :, :head_width]
    raw_keys = packed[:, :, head_width:2 * head_width]
    values = packed[:, :, 2 * head_width:]
    keys_norm = raw_keys * lax.rsqrt(lax.optimization_barrier(jnp.mean(raw_keys * raw_keys, axis=-1, keepdims=True)) + 1e-06)
    targets = values - keys_norm
    logits = jnp.einsum('thd,hd->ht', pieces, gate_f, precision=HIGH)
    rates = rate_f[:, None] * jax.nn.sigmoid(logits) / (MB * head_width)
    return (queries, keys_norm, targets, rates)

def blocked(array):
    head_count, tok_count = array.shape[:2]
    shaped = array.reshape((head_count, tok_count // MB, MB) + array.shape[2:])
    return jnp.moveaxis(shaped, 1, 0)

def run_chain(queries, keys_norm, targets, rates, start_weight):
    causal = jnp.tril(jnp.ones((MB, MB), queries.dtype))

    def minibatch_step(weight, blocks):
        q_block, k_block, y_block, e_block = blocks
        residual = jnp.einsum('hbd,hde->hbe', k_block, weight, precision=HIGH) - y_block
        scores = jnp.einsum('hbd,hcd->hbc', q_block, k_block, precision=HIGH) * causal * e_block[:, None, :]
        output = jnp.einsum('hbd,hde->hbe', q_block, weight, precision=HIGH) - jnp.einsum('hbc,hce->hbe', scores, residual, precision=HIGH)
        weight_next = weight - jnp.einsum('hbd,hbe->hde', k_block * e_block[:, :, None], residual, precision=HIGH)
        return (weight_next, output)
    blocks = (blocked(queries), blocked(keys_norm), blocked(targets), blocked(rates))
    end_weight, outputs = lax.scan(minibatch_step, start_weight, blocks)
    head_count, tok_count, head_width = queries.shape
    outputs = jnp.moveaxis(outputs, 0, 1).reshape(head_count, tok_count, head_width)
    return (outputs, end_weight)

def finish(tokens_f, outputs, gain_f):
    head_count, tok_count, head_width = outputs.shape
    centred = outputs - lax.optimization_barrier(jnp.mean(outputs, axis=-1, keepdims=True))
    normed = centred * lax.rsqrt(lax.optimization_barrier(jnp.mean(centred * centred, axis=-1, keepdims=True)) + 1e-05)
    mixed = normed * gain_f[:, None, :]
    return tokens_f + jnp.moveaxis(mixed, 0, 1).reshape(tok_count, head_count * head_width)

def reference(segment_input, views, gate_vec, base_rate, norm_gain, init_weight, out_grad):

    def section(packed):
        tokens, view_w, gate_w, rate_w, gain_w, start_w, cotangent = packed

        def forward(view_f, gate_f, rate_f, gain_f, start_f, tokens_f):
            queries, keys_norm, targets, rates = head_views(view_f, gate_f, rate_f, tokens_f)
            outputs, end_weight = run_chain(queries, keys_norm, targets, rates, start_f)
            return finish(tokens_f, outputs, gain_f)
        result, pullback = jax.vjp(forward, view_w.astype(jnp.float32), gate_w, rate_w, gain_w, start_w, tokens.astype(jnp.float32))
        grads = pullback(cotangent.astype(jnp.float32))
        return (result.astype(jnp.bfloat16), grads[0], grads[1], grads[2], grads[3], grads[4], grads[5].astype(jnp.bfloat16))
    outs = lax.map(section, (segment_input, views, gate_vec, base_rate, norm_gain, init_weight, out_grad))
    next_input = jnp.roll(outs[0], 1, axis=0)
    input_grad = jnp.roll(outs[6], -1, axis=0)
    return (next_input, outs[1], outs[2], outs[3], outs[4], outs[5], input_grad)
```

```python
import functools

import jax
import jax.numpy as jnp
from jax import lax
from jax.experimental import pallas as pl
from jax.experimental.pallas import tpu as pltpu
from jax.sharding import PartitionSpec as P

MB = 16
F32 = jnp.float32
BF16 = jnp.bfloat16
MESH = pl.DeviceIdType.MESH
NN = (((1,), (0,)), ((), ()))
NT = (((1,), (1,)), ((), ()))
TN = (((0,), (0,)), ((), ()))


def dot(left, right, dims):
    return lax.dot_general(left, right, dims, preferred_element_type=F32)


def split(value):
    high = value.astype(BF16)
    low = (value - high.astype(F32)).astype(BF16)
    return high, low


def cat(parts, axis):
    return jnp.concatenate(parts, axis=axis)


def stack(left, right, axis):
    return cat([left[0], right[0]], axis), cat([left[1], right[1]], axis)


def product(left, right, dims):
    left_axis, right_axis = dims[0][0][0], dims[0][1][0]
    left_both = cat(left, left_axis)
    wide = cat(right, 1 - right_axis)
    result = dot(left_both, cat([wide, wide], right_axis), dims)
    columns = result.shape[1] // 2
    return result[:, :columns] + result[:, columns:]


def row_mean(value):
    return jnp.mean(value, axis=-1, keepdims=True)


def fill_masks(ref, size):
    rows = lax.broadcasted_iota(jnp.int32, (size, size), 0)
    columns = lax.broadcasted_iota(jnp.int32, (size, size), 1)
    chosen = [rows >= columns, (rows // MB) > (columns // MB), rows == columns]
    block = MB
    while block < size:
        same = (rows // (2 * block)) == (columns // (2 * block))
        chosen.append(same & ((rows // block) > (columns // block)))
        block *= 2
    for index, mask in enumerate(chosen):
        ref[index] = jnp.where(mask, 1.0, 0.0).astype(F32)


def levels_of(size):
    levels, block = 0, MB
    while block < size:
        levels, block = levels + 1, 2 * block
    return levels


def together(streams):
    streams = list(streams)
    while streams:
        alive = []
        for stream in streams:
            try:
                next(stream)
                alive.append(stream)
            except StopIteration:
                pass
        streams = alive


def kernel(
    count, sections, heads, size, width,
    x_ref, og_ref, views_ref, gate_ref, rate_ref, gain_ref, init_ref,
    next_ref, vgrad_ref, ggrad_ref, rgrad_ref, ngrad_ref, igrad_ref, prev_ref,
    view_buf, x_buf, og_buf, out_buf, dx_buf, masks,
    qs, ks, krs, qes, as_, ss, ts, fs, rs, dzs, ws, gs,
    kf, bs, sbs, os_, v0s, ls, ns, invs, sigs, rstds,
    state, w_out, g_in, g_out, total, total_in, small, small_in,
    load_sem, x_send, x_recv, og_send, og_recv, out_send, out_recv, dx_send, dx_recv,
    w_send, w_recv, g_send, g_recv, i_recv, t_send, t_recv,
):
    me = lax.axis_index("ctx")
    section = lax.axis_index("segment")
    after = (section + 1) % sections
    before_me = (section + sections - 1) % sections
    chunks = count // 2
    late = me // chunks
    rank = me % chunks
    first = late * chunks
    partner = (me + chunks) % count
    lanes = 2 * heads

    def head_of(l, place):
        return ((1 - l // heads) * chunks + place) * heads + l % heads

    def columns(head):
        return pl.ds(pl.multiple_of(head * width, width), width)

    def mine(l):
        return head_of(l, rank)

    loads = []
    for block in range(2):
        start = mine(block * heads)
        here = pl.ds(block * heads, heads)
        loads.append(pltpu.make_async_copy(views_ref.at[0, pl.ds(start, heads)], view_buf.at[here], load_sem.at[block]))

    def load_state(block):
        here = pl.ds(block * heads, heads)
        return pltpu.make_async_copy(
            init_ref.at[0, pl.ds(mine(block * heads), heads)], state.at[here], w_recv.at[block]
        )

    def own(source, target, receive, l):
        return pltpu.make_async_copy(
            source.at[0, :, columns(mine(l))], target.at[l, rank], receive.at[l]
        )

    for load in loads:
        load.start()
    for l in range(lanes):
        own(x_ref, x_buf, x_recv, l).start()
        own(og_ref, og_buf, og_recv, l).start()

    @pl.when(late == 0)
    def _():
        for block in range(2):
            load_state(block).start()

    barrier = pltpu.get_barrier_semaphore()
    for step in range(1, chunks):
        pl.semaphore_signal(
            barrier, inc=1, device_id=(section, first + (rank + step) % chunks), device_id_type=MESH
        )
    pl.semaphore_signal(barrier, inc=1, device_id=(section, partner), device_id_type=MESH)
    for c in range(chunks):
        pl.semaphore_signal(barrier, inc=1, device_id=(after, first + c), device_id_type=MESH)
        pl.semaphore_signal(barrier, inc=1, device_id=(before_me, first + c), device_id_type=MESH)
    pl.semaphore_wait(barrier, 3 * chunks)

    def remote(source, target, send, receive, device):
        return pltpu.make_async_remote_copy(
            src_ref=source, dst_ref=target, send_sem=send, recv_sem=receive,
            device_id=device, device_id_type=MESH,
        )

    def settle(ref, semaphore):
        pltpu.make_async_copy(ref, ref, semaphore).wait()

    def spread(source, target, send, receive, l):
        for step in range(1, chunks):
            peer = (rank + step) % chunks
            remote(
                source.at[0, :, columns(head_of(l, peer))], target.at[l, rank],
                send.at[0], receive.at[l], (section, first + peer),
            ).start()

    def collect(source, target, send, receive, l, c, to):
        remote(
            source.at[l, c], target.at[0, :, columns(mine(l))],
            send.at[0], receive.at[0], (to, first + c),
        ).start()

    for l in range(lanes):
        spread(x_ref, x_buf, x_send, x_recv, l)
    for load in loads:
        load.wait()
    scale = 1.0 / (MB * width)
    levels = levels_of(size)
    fill_masks(masks, size)

    def gate_of(l):
        return gate_ref[0, pl.ds(mine(l), 1), :]

    def gain_of(l):
        return gain_ref[0, pl.ds(mine(l), 1), :]

    def base_of(l):
        lane = lax.broadcasted_iota(jnp.int32, rate_ref.shape, 1)
        return jnp.sum(jnp.where(lane == mine(l), rate_ref[...], 0.0), axis=1, keepdims=True)

    def put(ref, l, c, pair):
        ref[l, c, 0] = pair[0]
        ref[l, c, 1] = pair[1]

    def get(ref, l, c):
        return ref[l, c, 0], ref[l, c, 1]

    def prepare(l, c):
        x = x_buf[l, c]
        packed = dot(x, view_buf[l], NN)
        yield
        q = packed[:, :width]
        raw = packed[:, width : 2 * width]
        inv = lax.rsqrt(row_mean(raw * raw) + 1e-06)
        k = raw * inv
        y = packed[:, 2 * width :] - k
        logit = jnp.sum(x.astype(F32) * gate_of(l), axis=-1, keepdims=True)
        sig = jax.nn.sigmoid(logit)
        kr = k * (base_of(l) * sig * scale)
        k2, q2, kr2 = split(k), split(q), split(kr)
        y2 = split(y)
        yield
        grams = product(stack(k2, q2, 0), kr2, NT)
        yield
        scores = split(masks[0] * grams[size:])
        strict = grams[:size]
        inverse = masks[2] - masks[3] * strict if levels else masks[2]
        t2 = split(inverse)
        for level in range(1, levels):
            half_way = product(t2, split(masks[3 + level] * strict), NN)
            yield
            inverse = inverse - product(split(half_way), t2, NN)
            t2 = split(inverse)
            yield
        ab = product(t2, stack(k2, y2, 1), NN)
        yield
        ab2 = split(ab)
        sab = product(scores, ab2, NN)
        fo = product(kr2, ab2, TN)
        yield
        put(qs, l, c, q2)
        put(ks, l, c, k2)
        put(krs, l, c, kr2)
        put(qes, l, c, split(q - sab[:, :width]))
        put(as_, l, c, (ab2[0][:, :width], ab2[1][:, :width]))
        put(ss, l, c, scores)
        put(ts, l, c, t2)
        put(fs, l, c, split(fo[:, :width]))
        kf[l, c] = k
        bs[l, c] = ab[:, width:]
        sbs[l, c] = sab[:, width:]
        os_[l, c] = fo[:, width:]
        invs[l, c] = inv
        sigs[l, c] = sig

    def emit(l, c):
        moved = product(stack(get(qes, l, c), get(as_, l, c), 0), get(ws, l, c), NN)
        yield
        z = moved[:size] + sbs[l, c]
        put(rs, l, c, split(moved[size:] - bs[l, c]))
        centred = z - row_mean(z)
        yield
        rstd = lax.rsqrt(row_mean(centred * centred) + 1e-05)
        normed = centred * rstd
        out_buf[l, c] = (x_buf[l, c].astype(F32) + gain_of(l) * normed).astype(BF16)
        ns[l, c] = normed
        rstds[l, c] = rstd
        yield

    def receive_grad(l, c, gains):
        dout = og_buf[l, c].astype(F32)
        normed = ns[l, c]
        gains.append(jnp.sum(dout * normed, axis=0, keepdims=True))
        dn = dout * gain_of(l)
        dz = rstds[l, c] * (dn - row_mean(dn) - normed * row_mean(dn * normed))
        dz2 = split(dz)
        put(dzs, l, c, dz2)
        yield
        back = product(stack(get(qes, l, c), get(ss, l, c), 1), dz2, TN)
        ls[l, c] = back[:width]
        v0s[l, c] = back[width:]
        yield

    def gradients(l, c, found):
        g2 = get(gs, l, c)
        kr2, w2, r2, dz2 = get(krs, l, c), get(ws, l, c), get(rs, l, c), get(dzs, l, c)
        v = v0s[l, c] + product(kr2, g2, NN)
        yield
        du = -product(get(ts, l, c), split(v), TN)
        yield
        both = stack(dz2, split(du), 0)
        inner = product(both, r2, NT)
        yield
        d2 = stack(split(-masks[0] * inner[:size]), split(-masks[1] * inner[size:]), 0)
        dqk = product(both, w2, NT) + product(d2, kr2, NN)
        yield
        dkr = product(d2, stack(get(qs, l, c), get(ks, l, c), 0), TN) - product(r2, g2, NT)
        yield
        sig, inv, k, base = sigs[l, c], invs[l, c], kf[l, c], base_of(l)
        rate_factor = sig * scale
        dk = dqk[size:] + (base * rate_factor) * dkr + du
        draw = inv * (dk - k * row_mean(dk * k))
        drate = jnp.sum(dkr * k, axis=-1, keepdims=True) * rate_factor
        dlogit = drate * base * (1.0 - sig)
        x = x_buf[l, c]
        packed = split(cat([dqk[:size], draw, -du], 1))
        found.append((
            jnp.sum(dlogit * x.astype(F32), axis=0, keepdims=True),
            jnp.sum(drate, axis=0, keepdims=True),
            dot(cat([x, x], 0), cat(packed, 0), TN),
        ))
        yield
        views = view_buf[l]
        dx = dot(packed[0], views, NT) + dot(packed[1], views, NT)
        dx = dx + og_buf[l, c].astype(F32) + dlogit * gate_of(l)
        dx_buf[l, c] = dx.astype(BF16)

    every = range(chunks)
    pairing = 2 if heads % 2 == 0 else 1

    def prepare_lanes(some):
        for l in some:
            settle(x_buf.at[l], x_recv.at[l])
        for start in range(0, chunks, 2):
            together(prepare(l, c) for l in some for c in range(start, min(start + 2, chunks)))

    def advance(some, last):
        held = [state[l] for l in some]
        for c in every:
            for h, l in enumerate(some):
                pair = split(held[h])
                put(ws, l, c, pair)
                if c < chunks - 1 or last:
                    held[h] = held[h] - product(get(fs, l, c), pair, NN) + os_[l, c]
        return held

    def retreat(some, held):
        for c in reversed(every):
            if held is None:
                for l in some:
                    zero = jnp.zeros((width, width), BF16)
                    put(gs, l, c, (zero, zero))
                held = [ls[l, c] for l in some]
                continue
            for h, l in enumerate(some):
                pair = split(held[h])
                put(gs, l, c, pair)
                held[h] = held[h] - product(get(fs, l, c), pair, TN) + ls[l, c]
        for h, l in enumerate(some):
            g_out[l] = held[h]

    def emit_lanes(some):
        for start in range(0, chunks, 2):
            cs = range(start, min(start + 2, chunks))
            together(emit(l, c) for l in some for c in cs)
            for l in some:
                for c in cs:
                    collect(out_buf, next_ref, out_send, out_recv, l, c, after)

    def receive_lanes(some):
        gains = [[] for _ in some]
        for start in range(0, chunks, 2):
            together(
                receive_grad(l, c, gains[h])
                for h, l in enumerate(some)
                for c in range(start, min(start + 2, chunks))
            )
        for h, l in enumerate(some):
            small[l, 1:2, :] = sum(gains[h])

    def gradient_lanes(some):
        found = [[] for _ in some]
        for start in range(0, chunks, 2):
            cs = range(start, min(start + 2, chunks))
            together(gradients(l, c, found[h]) for h, l in enumerate(some) for c in cs)
            for l in some:
                for c in cs:
                    collect(dx_buf, prev_ref, dx_send, dx_recv, l, c, before_me)
        for h, l in enumerate(some):
            small[l, 0:1, :] = sum(item[0] for item in found[h])
            small[l, 2:3, :] = jnp.broadcast_to(sum(item[1] for item in found[h]), (1, width))
            total[l] = sum(item[2] for item in found[h])

    def lanes_of(block):
        return [block * heads + h for h in range(heads)]

    small[...] = jnp.zeros_like(small)

    def wait_state(block):
        here = state.at[pl.ds(block * heads, heads)]
        settle(here, w_recv.at[block])

    def here_of(ref, block):
        return ref.at[pl.ds(block * heads, heads)]

    def send_state(block):
        return remote(here_of(w_out, block), here_of(state, block), w_send.at[0], w_recv.at[block], (section, partner))

    def send_grad(block):
        return remote(here_of(g_out, block), here_of(g_in, block), g_send.at[0], g_recv.at[block], (section, partner))

    def send_init(block):
        return remote(here_of(g_out, block), igrad_ref.at[0], g_send.at[0], i_recv.at[0], (section, partner))

    def first_step(block, carry):
        some = lanes_of(block)
        prepare_lanes(some)

        @pl.when(late == 0)
        def _():
            wait_state(block)
            held = advance(some, True)
            for h, l in enumerate(some):
                w_out[l] = held[h]
            send_state(block).start()

        for l in some:
            spread(og_ref, og_buf, og_send, og_recv, l)
        return carry

    lax.fori_loop(0, 2, first_step, 0)

    def second_step(block, carry):
        some = lanes_of(block)

        @pl.when(late == 1)
        def _():
            wait_state(block)
            advance(some, False)

        emit_lanes(some)
        for l in some:
            settle(og_buf.at[l], og_recv.at[l])
        receive_lanes(some)

        @pl.when(late == 1)
        def _():
            retreat(some, None)
            send_grad(block).start()

        return carry

    lax.fori_loop(0, 2, second_step, 0)

    def third_step(step, carry):
        block = (step + late) % 2
        some = lanes_of(block)

        @pl.when(late == 0)
        def _():
            settle(here_of(g_in, block), g_recv.at[block])
            retreat(some, [g_in[l] for l in some])

            @pl.when(block == 0)
            def _():
                send_init(block).start()

            @pl.when(block == 1)
            def _():
                igrad_ref[0] = g_out[heads:]

        gradient_lanes(some)

        @pl.when(step == 0)
        def _():
            remote(here_of(total, block), total_in, t_send.at[0], t_recv.at[0], (section, partner)).start()
            remote(here_of(small, block), small_in, t_send.at[1], t_recv.at[1], (section, partner)).start()

        return carry

    lax.fori_loop(0, 2, third_step, 0)

    settle(total_in, t_recv.at[0])
    settle(small_in, t_recv.at[1])
    kept = 1 - late
    for h in range(heads):
        l = kept * heads + h
        vgrad_ref[0, h] = total[l] + total_in[h]
        sums = small[l] + small_in[h]
        ggrad_ref[0, h : h + 1, :] = sums[0:1]
        ngrad_ref[0, h : h + 1, :] = sums[1:2]
        rgrad_ref[:, h : h + 1] = sums[2:3, 0:1]

    settle(x_buf.at[:, pl.ds(0, chunks - 1)], x_send.at[0])
    settle(og_buf.at[:, pl.ds(0, chunks - 1)], og_send.at[0])
    settle(total_in, t_send.at[0])
    settle(small_in, t_send.at[1])

    @pl.when(late == 0)
    def _():
        settle(w_out, w_send.at[0])
        settle(here_of(g_out, 0), g_send.at[0])

    @pl.when(late == 1)
    def _():
        settle(g_out, g_send.at[0])
        settle(igrad_ref.at[0], i_recv.at[0])

    settle(out_buf, out_send.at[0])
    settle(dx_buf, dx_send.at[0])
    settle(next_ref, out_recv.at[0])
    settle(prev_ref, dx_recv.at[0])


def hand_over(*refs):
    number = (len(refs) - 1) // 2
    copies = [pltpu.make_async_copy(refs[i], refs[number + i], refs[-1].at[i]) for i in range(number)]
    for copy in copies:
        copy.start()
    for copy in copies:
        copy.wait()


def per_device(segment_input, views, gate_vec, base_rate, norm_gain, init_weight, out_grad):
    count = lax.axis_size("ctx")
    size, features = segment_input.shape[1:]
    every, width = gate_vec.shape[1:]
    heads = every // count
    lanes, chunks = 2 * heads, count // 2

    def shaped(shape, kind):
        return jax.ShapeDtypeStruct(shape, kind)

    vmem = pl.BlockSpec(memory_space=pltpu.VMEM)
    hbm = pl.BlockSpec(memory_space=pl.ANY)

    def pairs(rows, columns):
        return pltpu.VMEM((lanes, chunks, 2, rows, columns), BF16)

    def floats(rows, columns):
        return pltpu.VMEM((lanes, chunks, rows, columns), F32)

    tokens = pltpu.VMEM((lanes, chunks, size, width), BF16)
    matrix = pltpu.VMEM((lanes, width, width), F32)
    semaphores = [2, 1, lanes, 1, lanes, 1, 1, 1, 1, 1, 2, 1, 2, 1, 2, 2]

    results = pl.pallas_call(
        functools.partial(kernel, count, lax.axis_size("segment"), heads, size, width),
        out_shape=(
            shaped((1, size, features), BF16),
            shaped((1, heads, width, 3 * width), F32),
            shaped((1, heads, width), F32),
            shaped((1, heads), F32),
            shaped((1, heads, width), F32),
            shaped((1, heads, width, width), F32),
            shaped((1, size, features), BF16),
        ),
        in_specs=[hbm, hbm, hbm, vmem, vmem, vmem, hbm],
        out_specs=(hbm,) + (vmem,) * 5 + (hbm,),
        scratch_shapes=[
            pltpu.VMEM((lanes, width, 3 * width), BF16),
            tokens, tokens, tokens, tokens,
            pltpu.VMEM((3 + levels_of(size), size, size), F32),
            pairs(size, width), pairs(size, width), pairs(size, width), pairs(size, width), pairs(size, width),
            pairs(size, size), pairs(size, size), pairs(width, width),
            pairs(size, width), pairs(size, width), pairs(width, width), pairs(width, width),
            floats(size, width), floats(size, width), floats(size, width), floats(width, width),
            floats(size, width), floats(width, width), floats(size, width),
            floats(size, 1), floats(size, 1), floats(size, 1),
            matrix, matrix, matrix, matrix,
            pltpu.VMEM((lanes, width, 3 * width), F32),
            pltpu.VMEM((heads, width, 3 * width), F32),
            pltpu.VMEM((lanes, 8, width), F32),
            pltpu.VMEM((heads, 8, width), F32),
            *[pltpu.SemaphoreType.DMA((number,)) for number in semaphores],
        ],
        compiler_params=pltpu.CompilerParams(
            vmem_limit_bytes=56 * 1024 * 1024, collective_id=0, has_side_effects=True
        ),
    )(
        segment_input, out_grad, views, gate_vec, base_rate, norm_gain, init_weight
    )
    return pl.pallas_call(
        hand_over,
        out_shape=tuple(shaped(value.shape, value.dtype) for value in results),
        in_specs=[hbm] * len(results),
        out_specs=(vmem,) * len(results),
        scratch_shapes=[pltpu.SemaphoreType.DMA((len(results),))],
    )(*results)


def solution(mesh):
    return jax.shard_map(
        per_device,
        mesh=mesh,
        in_specs=(
            P("segment", "ctx", None),
            P("segment", None, None, None),
            P("segment", None, None),
            P("segment", None),
            P("segment", None, None),
            P("segment", None, None, None),
            P("segment", "ctx", None),
        ),
        out_specs=(
            P("segment", "ctx", None),
            P("segment", "ctx", None, None),
            P("segment", "ctx", None),
            P("segment", "ctx"),
            P("segment", "ctx", None),
            P("segment", "ctx", None, None),
            P("segment", "ctx", None),
        ),
        check_vma=False,
    )
```

```python
import functools

import jax
import jax.numpy as jnp
from jax import lax
from jax.experimental import pallas as pl
from jax.experimental.pallas import tpu as pltpu
from jax.sharding import PartitionSpec as P

MB = 16
REACH = 120.0
F32 = jnp.float32
BF16 = jnp.bfloat16
MESH = pl.DeviceIdType.MESH
NN = (((1,), (0,)), ((), ()))
NT = (((1,), (1,)), ((), ()))
TN = (((0,), (0,)), ((), ()))


def dot(left, right, dims):
    return lax.dot_general(left, right, dims, preferred_element_type=F32)


def split(value):
    high = value.astype(BF16)
    low = (value - high.astype(F32)).astype(BF16)
    return high, low


def cat(parts, axis):
    return jnp.concatenate(parts, axis=axis)


def stack(left, right, axis):
    return cat([left[0], right[0]], axis), cat([left[1], right[1]], axis)


def product(left, right, dims):
    left_axis, right_axis = dims[0][0][0], dims[0][1][0]
    left_both = cat(left, left_axis)
    wide = cat(right, 1 - right_axis)
    result = dot(left_both, cat([wide, wide], right_axis), dims)
    columns = result.shape[1] // 2
    return result[:, :columns] + result[:, columns:]


def row_mean(value):
    return jnp.mean(value, axis=-1, keepdims=True)


def fill_masks(ref, size):
    rows = lax.broadcasted_iota(jnp.int32, (size, size), 0)
    columns = lax.broadcasted_iota(jnp.int32, (size, size), 1)
    chosen = [rows >= columns, (rows // MB) > (columns // MB), rows == columns]
    block = MB
    while block < size:
        same = (rows // (2 * block)) == (columns // (2 * block))
        chosen.append(same & ((rows // block) > (columns // block)))
        block *= 2
    for index, mask in enumerate(chosen):
        ref[index] = jnp.where(mask, 1.0, 0.0).astype(F32)


def levels_of(size):
    levels, block = 0, MB
    while block < size:
        levels, block = levels + 1, 2 * block
    return levels


def together(streams):
    streams = list(streams)
    while streams:
        alive = []
        for stream in streams:
            try:
                next(stream)
                alive.append(stream)
            except StopIteration:
                pass
        streams = alive


def kernel(
    count, sections, heads, size, width,
    x_ref, og_ref, views_ref, gate_ref, rate_ref, gain_ref, init_ref,
    next_ref, vgrad_ref, ggrad_ref, rgrad_ref, ngrad_ref, igrad_ref, prev_ref,
    view_buf, x_buf, og_buf, out_buf, dx_buf, masks,
    qs, ks, krs, qes, as_, ss, ts, fs, rs, dzs, ws, gs,
    kf, bs, sbs, os_, v0s, ls, ns, invs, sigs, rstds,
    init_buf, w_out, w_in, g_out, g_in, i_in, total, total_out, total_in, small, small_in,
    load_sem, x_send, x_recv, og_send, og_recv, out_send, out_recv, dx_send, dx_recv,
    w_send, w_recv, g_send, g_recv, i_recv, t_send, t_recv, s_send, s_recv,
):
    me = lax.axis_index("ctx")
    section = lax.axis_index("segment")
    after = (section + 1) % sections
    before_me = (section + sections - 1) % sections
    chunks = count // 2
    late = me // chunks
    rank = me % chunks
    first = late * chunks
    partner = (me + chunks) % count
    lanes = 2 * heads

    def head_of(l, place):
        return ((1 - l // heads) * chunks + place) * heads + l % heads

    def columns(head):
        return pl.ds(pl.multiple_of(head * width, width), width)

    def mine(l):
        return head_of(l, rank)

    loads = []
    for block in range(2):
        start = mine(block * heads)
        here = pl.ds(block * heads, heads)
        loads.append(pltpu.make_async_copy(views_ref.at[0, pl.ds(start, heads)], view_buf.at[here], load_sem.at[block]))
        loads.append(pltpu.make_async_copy(init_ref.at[0, pl.ds(start, heads)], init_buf.at[here], load_sem.at[2 + block]))

    def own(source, target, receive, l):
        return pltpu.make_async_copy(
            source.at[0, :, columns(mine(l))], target.at[l, rank], receive.at[l]
        )

    for load in loads:
        load.start()
    for l in range(lanes):
        own(x_ref, x_buf, x_recv, l).start()
        own(og_ref, og_buf, og_recv, l).start()

    barrier = pltpu.get_barrier_semaphore()
    for step in range(1, chunks):
        pl.semaphore_signal(
            barrier, inc=1, device_id=(section, first + (rank + step) % chunks), device_id_type=MESH
        )
    pl.semaphore_signal(barrier, inc=1, device_id=(section, partner), device_id_type=MESH)
    for c in range(chunks):
        pl.semaphore_signal(barrier, inc=1, device_id=(after, first + c), device_id_type=MESH)
        pl.semaphore_signal(barrier, inc=1, device_id=(before_me, first + c), device_id_type=MESH)
    pl.semaphore_wait(barrier, 3 * chunks)

    def remote(source, target, send, receive, device):
        return pltpu.make_async_remote_copy(
            src_ref=source, dst_ref=target, send_sem=send, recv_sem=receive,
            device_id=device, device_id_type=MESH,
        )

    def settle(ref, semaphore):
        pltpu.make_async_copy(ref, ref, semaphore).wait()

    def spread(source, target, send, receive, l):
        for step in range(1, chunks):
            peer = (rank + step) % chunks
            remote(
                source.at[0, :, columns(head_of(l, peer))], target.at[l, rank],
                send.at[0], receive.at[l], (section, first + peer),
            ).start()

    def collect(source, target, send, receive, l, c, to):
        remote(
            source.at[l, c], target.at[0, :, columns(mine(l))],
            send.at[0], receive.at[0], (to, first + c),
        ).start()

    for l in range(lanes):
        spread(x_ref, x_buf, x_send, x_recv, l)
    for load in loads:
        load.wait()
    scale = 1.0 / (MB * width)
    levels = levels_of(size)
    fill_masks(masks, size)

    def gate_of(l):
        return gate_ref[0, pl.ds(mine(l), 1), :]

    def gain_of(l):
        return gain_ref[0, pl.ds(mine(l), 1), :]

    def base_of(l):
        lane = lax.broadcasted_iota(jnp.int32, rate_ref.shape, 1)
        return jnp.sum(jnp.where(lane == mine(l), rate_ref[...], 0.0), axis=1, keepdims=True)

    def put(ref, l, c, pair):
        ref[l, c, 0] = pair[0]
        ref[l, c, 1] = pair[1]

    def get(ref, l, c):
        return ref[l, c, 0], ref[l, c, 1]

    def prepare(l, c):
        x = x_buf[l, c]
        packed = dot(x, view_buf[l], NN)
        yield
        q = packed[:, :width]
        raw = packed[:, width : 2 * width]
        inv = lax.rsqrt(row_mean(raw * raw) + 1e-06)
        k = raw * inv
        y = packed[:, 2 * width :] - k
        logit = jnp.sum(x.astype(F32) * gate_of(l), axis=-1, keepdims=True)
        sig = jax.nn.sigmoid(logit)
        kr = k * (base_of(l) * sig * scale)
        k2, q2, kr2 = split(k), split(q), split(kr)
        y2 = split(y)
        yield
        grams = product(stack(k2, q2, 0), kr2, NT)
        yield
        scores = split(masks[0] * grams[size:])
        strict = grams[:size]
        inverse = masks[2] - masks[3] * strict if levels else masks[2]
        t2 = split(inverse)
        for level in range(1, levels):
            half_way = product(t2, split(masks[3 + level] * strict), NN)
            yield
            inverse = inverse - product(split(half_way), t2, NN)
            t2 = split(inverse)
            yield
        ab = product(t2, stack(k2, y2, 1), NN)
        yield
        ab2 = split(ab)
        sab = product(scores, ab2, NN)
        fo = product(kr2, ab2, TN)
        yield
        put(qs, l, c, q2)
        put(ks, l, c, k2)
        put(krs, l, c, kr2)
        put(qes, l, c, split(q - sab[:, :width]))
        put(as_, l, c, (ab2[0][:, :width], ab2[1][:, :width]))
        put(ss, l, c, scores)
        put(ts, l, c, t2)
        put(fs, l, c, split(fo[:, :width]))
        kf[l, c] = k
        bs[l, c] = ab[:, width:]
        sbs[l, c] = sab[:, width:]
        os_[l, c] = fo[:, width:]
        invs[l, c] = inv
        sigs[l, c] = sig

    def emit(l, c):
        moved = product(stack(get(qes, l, c), get(as_, l, c), 0), get(ws, l, c), NN)
        yield
        z = moved[:size] + sbs[l, c]
        put(rs, l, c, split(moved[size:] - bs[l, c]))
        centred = z - row_mean(z)
        yield
        rstd = lax.rsqrt(row_mean(centred * centred) + 1e-05)
        normed = centred * rstd
        out_buf[l, c] = (x_buf[l, c].astype(F32) + gain_of(l) * normed).astype(BF16)
        ns[l, c] = normed
        rstds[l, c] = rstd
        yield

    def receive_grad(l, c, gains):
        dout = og_buf[l, c].astype(F32)
        normed = ns[l, c]
        gains.append(jnp.sum(dout * normed, axis=0, keepdims=True))
        dn = dout * gain_of(l)
        dz = rstds[l, c] * (dn - row_mean(dn) - normed * row_mean(dn * normed))
        dz2 = split(dz)
        put(dzs, l, c, dz2)
        yield
        back = product(stack(get(qes, l, c), get(ss, l, c), 1), dz2, TN)
        ls[l, c] = back[:width]
        v0s[l, c] = back[width:]
        yield

    def gradients(l, c, found):
        g2 = get(gs, l, c)
        kr2, w2, r2, dz2 = get(krs, l, c), get(ws, l, c), get(rs, l, c), get(dzs, l, c)
        v = v0s[l, c] + product(kr2, g2, NN)
        yield
        du = -product(get(ts, l, c), split(v), TN)
        yield
        both = stack(dz2, split(du), 0)
        inner = product(both, r2, NT)
        yield
        d2 = stack(split(-masks[0] * inner[:size]), split(-masks[1] * inner[size:]), 0)
        dqk = product(both, w2, NT) + product(d2, kr2, NN)
        yield
        dkr = product(d2, stack(get(qs, l, c), get(ks, l, c), 0), TN) - product(r2, g2, NT)
        yield
        sig, inv, k, base = sigs[l, c], invs[l, c], kf[l, c], base_of(l)
        rate_factor = sig * scale
        dk = dqk[size:] + (base * rate_factor) * dkr + du
        draw = inv * (dk - k * row_mean(dk * k))
        drate = jnp.sum(dkr * k, axis=-1, keepdims=True) * rate_factor
        dlogit = drate * base * (1.0 - sig)
        x = x_buf[l, c]
        packed = split(cat([dqk[:size], draw, -du], 1))
        found.append((
            jnp.sum(dlogit * x.astype(F32), axis=0, keepdims=True),
            jnp.sum(drate, axis=0, keepdims=True),
            dot(cat([x, x], 0), cat(packed, 0), TN),
        ))
        yield
        views = view_buf[l]
        dx = dot(packed[0], views, NT) + dot(packed[1], views, NT)
        dx = dx + og_buf[l, c].astype(F32) + dlogit * gate_of(l)
        dx_buf[l, c] = dx.astype(BF16)

    every = range(chunks)
    batches = [range(start, min(start + 4, chunks)) for start in range(0, chunks, 4)]

    def encode(value, ref):
        rows = value.shape[0]
        peak = (jnp.max(jnp.abs(value), axis=0, keepdims=True) * 1.01 + 1e-30).astype(BF16)
        level = jnp.exp2(jnp.abs(value) * (2 * REACH / peak.astype(F32)) - REACH)
        ref[:rows] = jnp.where(value < 0, -level, level).astype(BF16)
        ref[rows:] = jnp.broadcast_to(peak, (MB, value.shape[1]))

    def decode(ref):
        rows = ref.shape[0] - MB
        coded = ref[:rows].astype(F32)
        peak = ref[rows:].astype(F32)[:1]
        level = (jnp.log2(jnp.abs(coded)) + REACH) * (peak * (0.5 / REACH))
        return jnp.where(coded < 0, -level, level)

    def advance(l, held, last):
        for c in every:
            pair = split(held)
            put(ws, l, c, pair)
            if c < chunks - 1 or last:
                held = held - product(get(fs, l, c), pair, NN) + os_[l, c]
        return held

    def retreat(l, held):
        for c in reversed(every):
            if held is None:
                zero = jnp.zeros((width, width), BF16)
                put(gs, l, c, (zero, zero))
                held = ls[l, c]
                continue
            pair = split(held)
            put(gs, l, c, pair)
            held = held - product(get(fs, l, c), pair, TN) + ls[l, c]
        return held

    small[...] = jnp.zeros_like(small)

    def first_step(l, carry):
        settle(x_buf.at[l], x_recv.at[l])
        for batch in batches:
            together(prepare(l, c) for c in batch)

        @pl.when(late == 0)
        def _():
            encode(advance(l, init_buf[l], True), w_out.at[l])
            remote(w_out.at[l], w_in.at[l], w_send.at[0], w_recv.at[l], (section, partner)).start()

        spread(og_ref, og_buf, og_send, og_recv, l)
        return carry

    lax.fori_loop(0, lanes, first_step, 0)

    def second_step(l, carry):
        @pl.when(late == 1)
        def _():
            settle(w_in.at[l], w_recv.at[l])
            advance(l, decode(w_in.at[l]), False)

        for batch in batches:
            together(emit(l, c) for c in batch)
            for c in batch:
                collect(out_buf, next_ref, out_send, out_recv, l, c, after)
        settle(og_buf.at[l], og_recv.at[l])
        gains = []
        for batch in batches:
            together(receive_grad(l, c, gains) for c in batch)
        small[l, 1:2, :] = sum(gains)

        @pl.when(late == 1)
        def _():
            encode(retreat(l, None), g_out.at[l])
            remote(g_out.at[l], g_in.at[l], g_send.at[0], g_recv.at[l], (section, partner)).start()

        return carry

    lax.fori_loop(0, lanes, second_step, 0)

    def third_step(step, carry):
        l = (step + late * heads) % lanes
        slot = l % heads

        @pl.when(late == 0)
        def _():
            settle(g_in.at[l], g_recv.at[l])
            start = retreat(l, decode(g_in.at[l]))

            @pl.when(l < heads)
            def _():
                encode(start, g_out.at[l])
                remote(g_out.at[l], i_in.at[l], g_send.at[0], i_recv.at[l], (section, partner)).start()

            @pl.when(l >= heads)
            def _():
                igrad_ref[0, slot] = start

        found = []
        for batch in batches:
            together(gradients(l, c, found) for c in batch)
            for c in batch:
                collect(dx_buf, prev_ref, dx_send, dx_recv, l, c, before_me)
        small[l, 0:1, :] = sum(item[0] for item in found)
        small[l, 2:3, :] = jnp.broadcast_to(sum(item[1] for item in found), (1, width))
        whole = sum(item[2] for item in found)

        @pl.when(step < heads)
        def _():
            encode(whole, total_out.at[slot])
            remote(total_out.at[slot], total_in.at[slot], t_send.at[0], t_recv.at[slot], (section, partner)).start()
            remote(small.at[l], small_in.at[slot], s_send.at[0], s_recv.at[slot], (section, partner)).start()

        @pl.when(step >= heads)
        def _():
            total[slot] = whole

        return carry

    lax.fori_loop(0, lanes, third_step, 0)

    for h in range(heads):
        settle(total_in.at[h], t_recv.at[h])
        settle(small_in.at[h], s_recv.at[h])
        vgrad_ref[0, h] = total[h] + decode(total_in.at[h])
        sums = small[(1 - late) * heads + h] + small_in[h]
        ggrad_ref[0, h : h + 1, :] = sums[0:1]
        ngrad_ref[0, h : h + 1, :] = sums[1:2]
        rgrad_ref[:, h : h + 1] = sums[2:3, 0:1]

    @pl.when(late == 1)
    def _():
        for h in range(heads):
            settle(i_in.at[h], i_recv.at[h])
            igrad_ref[0, h] = decode(i_in.at[h])

    settle(x_buf.at[:, pl.ds(0, chunks - 1)], x_send.at[0])
    settle(og_buf.at[:, pl.ds(0, chunks - 1)], og_send.at[0])
    settle(total_out, t_send.at[0])
    settle(small_in, s_send.at[0])

    @pl.when(late == 0)
    def _():
        settle(w_out, w_send.at[0])
        settle(i_in, g_send.at[0])

    @pl.when(late == 1)
    def _():
        settle(g_out, g_send.at[0])

    settle(out_buf, out_send.at[0])
    settle(dx_buf, dx_send.at[0])
    settle(next_ref, out_recv.at[0])
    settle(prev_ref, dx_recv.at[0])


def hand_over(*refs):
    number = (len(refs) - 1) // 2
    copies = [pltpu.make_async_copy(refs[i], refs[number + i], refs[-1].at[i]) for i in range(number)]
    for copy in copies:
        copy.start()
    for copy in copies:
        copy.wait()


def per_device(segment_input, views, gate_vec, base_rate, norm_gain, init_weight, out_grad):
    count = lax.axis_size("ctx")
    size, features = segment_input.shape[1:]
    every, width = gate_vec.shape[1:]
    heads = every // count
    lanes, chunks = 2 * heads, count // 2

    def shaped(shape, kind):
        return jax.ShapeDtypeStruct(shape, kind)

    vmem = pl.BlockSpec(memory_space=pltpu.VMEM)
    hbm = pl.BlockSpec(memory_space=pl.ANY)

    def pairs(rows, columns):
        return pltpu.VMEM((lanes, chunks, 2, rows, columns), BF16)

    def floats(rows, columns):
        return pltpu.VMEM((lanes, chunks, rows, columns), F32)

    tokens = pltpu.VMEM((lanes, chunks, size, width), BF16)
    matrix = pltpu.VMEM((lanes, width, width), F32)
    semaphores = [4, 1, lanes, 1, lanes, 1, 1, 1, 1, 1, lanes, 1, lanes, heads, 1, heads, 1, heads]
    coded = pltpu.VMEM((lanes, width + MB, width), BF16)
    wide = pltpu.VMEM((heads, width + MB, 3 * width), BF16)

    results = pl.pallas_call(
        functools.partial(kernel, count, lax.axis_size("segment"), heads, size, width),
        out_shape=(
            shaped((1, size, features), BF16),
            shaped((1, heads, width, 3 * width), F32),
            shaped((1, heads, width), F32),
            shaped((1, heads), F32),
            shaped((1, heads, width), F32),
            shaped((1, heads, width, width), F32),
            shaped((1, size, features), BF16),
        ),
        in_specs=[hbm, hbm, hbm, vmem, vmem, vmem, hbm],
        out_specs=(hbm,) + (vmem,) * 5 + (hbm,),
        scratch_shapes=[
            pltpu.VMEM((lanes, width, 3 * width), BF16),
            tokens, tokens, tokens, tokens,
            pltpu.VMEM((3 + levels_of(size), size, size), F32),
            pairs(size, width), pairs(size, width), pairs(size, width), pairs(size, width), pairs(size, width),
            pairs(size, size), pairs(size, size), pairs(width, width),
            pairs(size, width), pairs(size, width), pairs(width, width), pairs(width, width),
            floats(size, width), floats(size, width), floats(size, width), floats(width, width),
            floats(size, width), floats(width, width), floats(size, width),
            floats(size, 1), floats(size, 1), floats(size, 1),
            matrix, coded, coded, coded, coded,
            pltpu.VMEM((heads, width + MB, width), BF16),
            pltpu.VMEM((heads, width, 3 * width), F32),
            wide, wide,
            pltpu.VMEM((lanes, 8, width), F32),
            pltpu.VMEM((heads, 8, width), F32),
            *[pltpu.SemaphoreType.DMA((number,)) for number in semaphores],
        ],
        compiler_params=pltpu.CompilerParams(
            vmem_limit_bytes=56 * 1024 * 1024, collective_id=0, has_side_effects=True
        ),
    )(
        segment_input, out_grad, views, gate_vec, base_rate, norm_gain, init_weight
    )
    return pl.pallas_call(
        hand_over,
        out_shape=tuple(shaped(value.shape, value.dtype) for value in results),
        in_specs=[hbm] * len(results),
        out_specs=(vmem,) * len(results),
        scratch_shapes=[pltpu.SemaphoreType.DMA((len(results),))],
    )(*results)


def solution(mesh):
    return jax.shard_map(
        per_device,
        mesh=mesh,
        in_specs=(
            P("segment", "ctx", None),
            P("segment", None, None, None),
            P("segment", None, None),
            P("segment", None),
            P("segment", None, None),
            P("segment", None, None, None),
            P("segment", "ctx", None),
        ),
        out_specs=(
            P("segment", "ctx", None),
            P("segment", "ctx", None, None),
            P("segment", "ctx", None),
            P("segment", "ctx"),
            P("segment", "ctx", None),
            P("segment", "ctx", None, None),
            P("segment", "ctx", None),
        ),
        check_vma=False,
    )
```

```python
import functools

import jax
import jax.numpy as jnp
from jax import lax
from jax.experimental import pallas as pl
from jax.experimental.pallas import tpu as pltpu
from jax.sharding import PartitionSpec as P

MB = 16
REACH = 120.0
F32 = jnp.float32
BF16 = jnp.bfloat16
MESH = pl.DeviceIdType.MESH
NN = (((1,), (0,)), ((), ()))
NT = (((1,), (1,)), ((), ()))
TN = (((0,), (0,)), ((), ()))


def dot(left, right, dims):
    return lax.dot_general(left, right, dims, preferred_element_type=F32)


def split(value):
    high = value.astype(BF16)
    low = (value - high.astype(F32)).astype(BF16)
    return high, low


def cat(parts, axis):
    return jnp.concatenate(parts, axis=axis)


def stack(left, right, axis):
    return cat([left[0], right[0]], axis), cat([left[1], right[1]], axis)


def product(left, right, dims):
    left_axis, right_axis = dims[0][0][0], dims[0][1][0]
    left_both = cat(left, left_axis)
    wide = cat(right, 1 - right_axis)
    result = dot(left_both, cat([wide, wide], right_axis), dims)
    columns = result.shape[1] // 2
    return result[:, :columns] + result[:, columns:]


def row_mean(value):
    return jnp.mean(value, axis=-1, keepdims=True)


def fill_masks(ref, size):
    rows = lax.broadcasted_iota(jnp.int32, (size, size), 0)
    columns = lax.broadcasted_iota(jnp.int32, (size, size), 1)
    chosen = [rows >= columns, (rows // MB) > (columns // MB), rows == columns]
    block = MB
    while block < size:
        same = (rows // (2 * block)) == (columns // (2 * block))
        chosen.append(same & ((rows // block) > (columns // block)))
        block *= 2
    for index, mask in enumerate(chosen):
        ref[index] = jnp.where(mask, 1.0, 0.0).astype(F32)


def levels_of(size):
    levels, block = 0, MB
    while block < size:
        levels, block = levels + 1, 2 * block
    return levels


def together(streams):
    streams = list(streams)
    while streams:
        alive = []
        for stream in streams:
            try:
                next(stream)
                alive.append(stream)
            except StopIteration:
                pass
        streams = alive


def kernel(
    count, sections, heads, size, width,
    x_ref, og_ref, views_ref, gate_src, rate_src, gain_src, init_ref,
    next_ref, vgrad_ref, ggrad_ref, rgrad_ref, ngrad_ref, igrad_ref, prev_ref,
    gate_ref, rate_ref, gain_ref, view_buf, x_buf, og_buf, out_buf, dx_buf, masks,
    qs, ks, krs, qes, as_, ss, ts, fs, rs, dzs, ws, gs,
    kf, bs, sbs, os_, v0s, ls, ns, invs, sigs, rstds,
    init_buf, w_out, w_in, g_out, g_in, i_in, total, total_out, total_in, small, small_in,
    load_sem, own_sem, x_send, x_recv, og_send, og_recv, out_send, out_recv, dx_send, dx_recv,
    w_send, w_recv, g_send, g_recv, i_recv, t_send, t_recv, s_send, s_recv,
):
    me = lax.axis_index("ctx")
    section = lax.axis_index("segment")
    after = (section + 1) % sections
    before_me = (section + sections - 1) % sections
    chunks = count // 2
    late = me // chunks
    rank = me % chunks
    first = late * chunks
    partner = (me + chunks) % count
    lanes = 2 * heads

    def head_of(l, place):
        return ((1 - l // heads) * chunks + place) * heads + l % heads

    def columns(head):
        return pl.ds(pl.multiple_of(head * width, width), width)

    def mine(l):
        return head_of(l, rank)

    loads = []
    for block in range(2):
        start = mine(block * heads)
        here = pl.ds(block * heads, heads)
        loads.append(pltpu.make_async_copy(views_ref.at[0, pl.ds(start, heads)], view_buf.at[here], load_sem.at[block]))
        loads.append(pltpu.make_async_copy(init_ref.at[0, pl.ds(start, heads)], init_buf.at[here], load_sem.at[2 + block]))

    for index, (source, target) in enumerate(((gate_src, gate_ref), (rate_src, rate_ref), (gain_src, gain_ref))):
        loads.append(pltpu.make_async_copy(source, target, load_sem.at[4 + index]))

    def own(source, target, receive, l):
        return pltpu.make_async_copy(
            source.at[0, :, columns(mine(l))], target.at[l, rank], receive
        )

    barrier = pltpu.get_barrier_semaphore()
    for step in range(1, chunks):
        pl.semaphore_signal(
            barrier, inc=1, device_id=(section, first + (rank + step) % chunks), device_id_type=MESH
        )
    pl.semaphore_signal(barrier, inc=1, device_id=(section, partner), device_id_type=MESH)
    for c in range(chunks):
        pl.semaphore_signal(barrier, inc=1, device_id=(after, first + c), device_id_type=MESH)
        pl.semaphore_signal(barrier, inc=1, device_id=(before_me, first + c), device_id_type=MESH)
    for load in loads:
        load.start()
    for l in range(lanes):
        own(x_ref, x_buf, own_sem.at[0], l).start()
        own(og_ref, og_buf, own_sem.at[1], l).start()

    def remote(source, target, send, receive, device):
        return pltpu.make_async_remote_copy(
            src_ref=source, dst_ref=target, send_sem=send, recv_sem=receive,
            device_id=device, device_id_type=MESH,
        )

    def settle(ref, semaphore):
        pltpu.make_async_copy(ref, ref, semaphore).wait()

    def spread(source, target, send, receive, l):
        for step in range(1, chunks):
            peer = (rank + step) % chunks
            remote(
                source.at[0, :, columns(head_of(l, peer))], target.at[l, rank],
                send.at[0], receive.at[l], (section, first + peer),
            ).start()

    def collect(source, target, send, receive, l, c, to):
        remote(
            source.at[l, c], target.at[0, :, columns(mine(l))],
            send.at[0], receive.at[0], (to, first + c),
        ).start()

    pl.semaphore_wait(barrier, 3 * chunks)
    for l in range(lanes):
        spread(x_ref, x_buf, x_send, x_recv, l)
    for load in loads:
        load.wait()
    scale = 1.0 / (MB * width)
    levels = levels_of(size)
    fill_masks(masks, size)

    def gate_of(l):
        return gate_ref[0, pl.ds(mine(l), 1), :]

    def gain_of(l):
        return gain_ref[0, pl.ds(mine(l), 1), :]

    def base_of(l):
        lane = lax.broadcasted_iota(jnp.int32, rate_ref.shape, 1)
        return jnp.sum(jnp.where(lane == mine(l), rate_ref[...], 0.0), axis=1, keepdims=True)

    def put(ref, l, c, pair):
        ref[l, c, 0] = pair[0]
        ref[l, c, 1] = pair[1]

    def get(ref, l, c):
        return ref[l, c, 0], ref[l, c, 1]

    def prepare(l, c):
        x = x_buf[l, c]
        packed = dot(x, view_buf[l], NN)
        yield
        q = packed[:, :width]
        raw = packed[:, width : 2 * width]
        inv = lax.rsqrt(row_mean(raw * raw) + 1e-06)
        k = raw * inv
        y = packed[:, 2 * width :] - k
        logit = jnp.sum(x.astype(F32) * gate_of(l), axis=-1, keepdims=True)
        sig = jax.nn.sigmoid(logit)
        kr = k * (base_of(l) * sig * scale)
        k2, q2, kr2 = split(k), split(q), split(kr)
        y2 = split(y)
        yield
        grams = product(stack(k2, q2, 0), kr2, NT)
        yield
        scores = split(masks[0] * grams[size:])
        strict = grams[:size]
        inverse = masks[2] - masks[3] * strict if levels else masks[2]
        t2 = split(inverse)
        for level in range(1, levels):
            half_way = product(t2, split(masks[3 + level] * strict), NN)
            yield
            inverse = inverse - product(split(half_way), t2, NN)
            t2 = split(inverse)
            yield
        ab = product(t2, stack(k2, y2, 1), NN)
        yield
        ab2 = split(ab)
        sab = product(scores, ab2, NN)
        fo = product(kr2, ab2, TN)
        yield
        put(qs, l, c, q2)
        put(ks, l, c, k2)
        put(krs, l, c, kr2)
        put(qes, l, c, split(q - sab[:, :width]))
        put(as_, l, c, (ab2[0][:, :width], ab2[1][:, :width]))
        put(ss, l, c, scores)
        put(ts, l, c, t2)
        put(fs, l, c, split(fo[:, :width]))
        kf[l, c] = k
        bs[l, c] = ab[:, width:]
        sbs[l, c] = sab[:, width:]
        os_[l, c] = fo[:, width:]
        invs[l, c] = inv
        sigs[l, c] = sig

    def emit(l, c):
        moved = product(stack(get(qes, l, c), get(as_, l, c), 0), get(ws, l, c), NN)
        yield
        z = moved[:size] + sbs[l, c]
        put(rs, l, c, split(moved[size:] - bs[l, c]))
        centred = z - row_mean(z)
        yield
        rstd = lax.rsqrt(row_mean(centred * centred) + 1e-05)
        normed = centred * rstd
        out_buf[l, c] = (x_buf[l, c].astype(F32) + gain_of(l) * normed).astype(BF16)
        ns[l, c] = normed
        rstds[l, c] = rstd
        yield

    def receive_grad(l, c, gains):
        dout = og_buf[l, c].astype(F32)
        normed = ns[l, c]
        gains.append(jnp.sum(dout * normed, axis=0, keepdims=True))
        dn = dout * gain_of(l)
        dz = rstds[l, c] * (dn - row_mean(dn) - normed * row_mean(dn * normed))
        dz2 = split(dz)
        put(dzs, l, c, dz2)
        yield
        back = product(stack(get(qes, l, c), get(ss, l, c), 1), dz2, TN)
        ls[l, c] = back[:width]
        v0s[l, c] = back[width:]
        yield

    def gradients(l, c, found):
        g2 = get(gs, l, c)
        kr2, w2, r2, dz2 = get(krs, l, c), get(ws, l, c), get(rs, l, c), get(dzs, l, c)
        v = v0s[l, c] + product(kr2, g2, NN)
        yield
        du = -product(get(ts, l, c), split(v), TN)
        yield
        both = stack(dz2, split(du), 0)
        inner = product(both, r2, NT)
        yield
        d2 = stack(split(-masks[0] * inner[:size]), split(-masks[1] * inner[size:]), 0)
        dqk = product(both, w2, NT) + product(d2, kr2, NN)
        yield
        dkr = product(d2, stack(get(qs, l, c), get(ks, l, c), 0), TN) - product(r2, g2, NT)
        yield
        sig, inv, k, base = sigs[l, c], invs[l, c], kf[l, c], base_of(l)
        rate_factor = sig * scale
        dk = dqk[size:] + (base * rate_factor) * dkr + du
        draw = inv * (dk - k * row_mean(dk * k))
        drate = jnp.sum(dkr * k, axis=-1, keepdims=True) * rate_factor
        dlogit = drate * base * (1.0 - sig)
        x = x_buf[l, c]
        packed = split(cat([dqk[:size], draw, -du], 1))
        found.append((
            jnp.sum(dlogit * x.astype(F32), axis=0, keepdims=True),
            jnp.sum(drate, axis=0, keepdims=True),
            dot(cat([x, x], 0), cat(packed, 0), TN),
        ))
        yield
        views = view_buf[l]
        dx = dot(packed[0], views, NT) + dot(packed[1], views, NT)
        dx = dx + og_buf[l, c].astype(F32) + dlogit * gate_of(l)
        dx_buf[l, c] = dx.astype(BF16)

    every = range(chunks)
    batches = [range(start, min(start + 4, chunks)) for start in range(0, chunks, 4)]

    def encode(value, ref):
        rows = value.shape[0]
        peak = (jnp.max(jnp.abs(value), axis=0, keepdims=True) * 1.01 + 1e-30).astype(BF16)
        level = jnp.exp2(jnp.abs(value) * (2 * REACH / peak.astype(F32)) - REACH)
        ref[:rows] = jnp.where(value < 0, -level, level).astype(BF16)
        ref[rows:] = jnp.broadcast_to(peak, (MB, value.shape[1]))

    def decode(ref):
        rows = ref.shape[0] - MB
        coded = ref[:rows].astype(F32)
        peak = ref[rows:].astype(F32)[:1]
        level = (jnp.log2(jnp.abs(coded)) + REACH) * (peak * (0.5 / REACH))
        return jnp.where(coded < 0, -level, level)

    def advance(l, held, last):
        for c in every:
            pair = split(held)
            put(ws, l, c, pair)
            if c < chunks - 1 or last:
                held = held - product(get(fs, l, c), pair, NN) + os_[l, c]
        return held

    def retreat(l, held):
        for c in reversed(every):
            if held is None:
                zero = jnp.zeros((width, width), BF16)
                put(gs, l, c, (zero, zero))
                held = ls[l, c]
                continue
            pair = split(held)
            put(gs, l, c, pair)
            held = held - product(get(fs, l, c), pair, TN) + ls[l, c]
        return held

    small[...] = jnp.zeros_like(small)
    settle(x_buf.at[:, 0], own_sem.at[0])
    together(prepare(l, rank) for l in range(lanes))

    def emit_all(l):
        for batch in batches:
            together(emit(l, c) for c in batch)
            for c in batch:
                collect(out_buf, next_ref, out_send, out_recv, l, c, after)

    def first_step(l, carry):
        settle(x_buf.at[l, pl.ds(0, chunks - 1)], x_recv.at[l])
        for batch in batches:
            together(prepare(l, (rank + 1 + c) % chunks) for c in batch if c < chunks - 1)

        @pl.when(late == 0)
        def _():
            encode(advance(l, init_buf[l], True), w_out.at[l])
            remote(w_out.at[l], w_in.at[l], w_send.at[0], w_recv.at[l], (section, partner)).start()
            emit_all(l)

        spread(og_ref, og_buf, og_send, og_recv, l)
        return carry

    lax.fori_loop(0, lanes, first_step, 0)
    settle(og_buf.at[:, 0], own_sem.at[1])

    def second_step(l, carry):
        @pl.when(late == 1)
        def _():
            settle(w_in.at[l], w_recv.at[l])
            advance(l, decode(w_in.at[l]), False)
            emit_all(l)

        settle(og_buf.at[l, pl.ds(0, chunks - 1)], og_recv.at[l])
        gains = []
        for batch in batches:
            together(receive_grad(l, c, gains) for c in batch)
        small[l, 1:2, :] = sum(gains)

        @pl.when(late == 1)
        def _():
            encode(retreat(l, None), g_out.at[l])
            remote(g_out.at[l], g_in.at[l], g_send.at[0], g_recv.at[l], (section, partner)).start()

        return carry

    lax.fori_loop(0, lanes, second_step, 0)

    def third_step(step, carry):
        l = (step + late * heads) % lanes
        slot = l % heads

        @pl.when(late == 0)
        def _():
            settle(g_in.at[l], g_recv.at[l])
            start = retreat(l, decode(g_in.at[l]))

            @pl.when(l < heads)
            def _():
                encode(start, g_out.at[l])
                remote(g_out.at[l], i_in.at[l], g_send.at[0], i_recv.at[l], (section, partner)).start()

            @pl.when(l >= heads)
            def _():
                igrad_ref[0, slot] = start

        found = []
        for batch in batches:
            together(gradients(l, c, found) for c in batch)
            for c in batch:
                collect(dx_buf, prev_ref, dx_send, dx_recv, l, c, before_me)
        small[l, 0:1, :] = sum(item[0] for item in found)
        small[l, 2:3, :] = jnp.broadcast_to(sum(item[1] for item in found), (1, width))
        whole = sum(item[2] for item in found)

        @pl.when(step < heads)
        def _():
            encode(whole, total_out.at[slot])
            remote(total_out.at[slot], total_in.at[slot], t_send.at[0], t_recv.at[slot], (section, partner)).start()
            remote(small.at[l], small_in.at[slot], s_send.at[0], s_recv.at[slot], (section, partner)).start()

        @pl.when(step >= heads)
        def _():
            total[slot] = whole

        return carry

    lax.fori_loop(0, lanes, third_step, 0)

    for h in range(heads):
        settle(total_in.at[h], t_recv.at[h])
        settle(small_in.at[h], s_recv.at[h])
        vgrad_ref[0, h] = total[h] + decode(total_in.at[h])
        sums = small[(1 - late) * heads + h] + small_in[h]
        ggrad_ref[0, h : h + 1, :] = sums[0:1]
        ngrad_ref[0, h : h + 1, :] = sums[1:2]
        rgrad_ref[:, h : h + 1] = sums[2:3, 0:1]

    @pl.when(late == 1)
    def _():
        for h in range(heads):
            settle(i_in.at[h], i_recv.at[h])
            igrad_ref[0, h] = decode(i_in.at[h])

    settle(x_buf.at[:, pl.ds(0, chunks - 1)], x_send.at[0])
    settle(og_buf.at[:, pl.ds(0, chunks - 1)], og_send.at[0])
    settle(total_out, t_send.at[0])
    settle(small_in, s_send.at[0])

    @pl.when(late == 0)
    def _():
        settle(w_out, w_send.at[0])
        settle(i_in, g_send.at[0])

    @pl.when(late == 1)
    def _():
        settle(g_out, g_send.at[0])

    settle(out_buf, out_send.at[0])
    settle(dx_buf, dx_send.at[0])
    settle(next_ref, out_recv.at[0])
    settle(prev_ref, dx_recv.at[0])


def hand_over(*refs):
    number = (len(refs) - 1) // 2
    copies = [pltpu.make_async_copy(refs[i], refs[number + i], refs[-1].at[i]) for i in range(number)]
    for copy in copies:
        copy.start()
    for copy in copies:
        copy.wait()


def per_device(segment_input, views, gate_vec, base_rate, norm_gain, init_weight, out_grad):
    count = lax.axis_size("ctx")
    size, features = segment_input.shape[1:]
    every, width = gate_vec.shape[1:]
    heads = every // count
    lanes, chunks = 2 * heads, count // 2

    def shaped(shape, kind):
        return jax.ShapeDtypeStruct(shape, kind)

    vmem = pl.BlockSpec(memory_space=pltpu.VMEM)
    hbm = pl.BlockSpec(memory_space=pltpu.HBM)

    def pairs(rows, columns):
        return pltpu.VMEM((lanes, chunks, 2, rows, columns), BF16)

    def floats(rows, columns):
        return pltpu.VMEM((lanes, chunks, rows, columns), F32)

    tokens = pltpu.VMEM((lanes, chunks, size, width), BF16)
    matrix = pltpu.VMEM((lanes, width, width), F32)
    semaphores = [7, 2, 1, lanes, 1, lanes, 1, 1, 1, 1, 1, lanes, 1, lanes, heads, 1, heads, 1, heads]
    coded = pltpu.VMEM((lanes, width + MB, width), BF16)
    wide = pltpu.VMEM((heads, width + MB, 3 * width), BF16)

    results = pl.pallas_call(
        functools.partial(kernel, count, lax.axis_size("segment"), heads, size, width),
        out_shape=(
            pltpu.VMEM((1, size, features), BF16),
            pltpu.VMEM((1, heads, width, 3 * width), F32),
            pltpu.VMEM((1, heads, width), F32),
            pltpu.VMEM((1, heads), F32),
            pltpu.VMEM((1, heads, width), F32),
            pltpu.VMEM((1, heads, width, width), F32),
            pltpu.VMEM((1, size, features), BF16),
        ),
        in_specs=[hbm] * 7,
        out_specs=(vmem,) * 7,
        scratch_shapes=[
            pltpu.VMEM(gate_vec.shape, F32),
            pltpu.VMEM(base_rate.shape, F32),
            pltpu.VMEM(norm_gain.shape, F32),
            pltpu.VMEM((lanes, width, 3 * width), BF16),
            tokens, tokens, tokens, tokens,
            pltpu.VMEM((3 + levels_of(size), size, size), F32),
            pairs(size, width), pairs(size, width), pairs(size, width), pairs(size, width), pairs(size, width),
            pairs(size, size), pairs(size, size), pairs(width, width),
            pairs(size, width), pairs(size, width), pairs(width, width), pairs(width, width),
            floats(size, width), floats(size, width), floats(size, width), floats(width, width),
            floats(size, width), floats(width, width), floats(size, width),
            floats(size, 1), floats(size, 1), floats(size, 1),
            matrix, coded, coded, coded, coded,
            pltpu.VMEM((heads, width + MB, width), BF16),
            pltpu.VMEM((heads, width, 3 * width), F32),
            wide, wide,
            pltpu.VMEM((lanes, 8, width), F32),
            pltpu.VMEM((heads, 8, width), F32),
            *[pltpu.SemaphoreType.DMA((number,)) for number in semaphores],
        ],
        compiler_params=pltpu.CompilerParams(
            vmem_limit_bytes=52 * 1024 * 1024, collective_id=0, has_side_effects=True
        ),
    )(*[
        pltpu.with_memory_space_constraint(value, pltpu.HBM)
        for value in (segment_input, out_grad, views, gate_vec, base_rate, norm_gain, init_weight)
    ])
    results = [pltpu.with_memory_space_constraint(value, pltpu.VMEM) for value in results]
    return pl.pallas_call(
        hand_over,
        out_shape=tuple(shaped(value.shape, value.dtype) for value in results),
        in_specs=[vmem] * len(results),
        out_specs=(hbm,) * len(results),
        scratch_shapes=[pltpu.SemaphoreType.DMA((len(results),))],
    )(*results)


def solution(mesh):
    return jax.shard_map(
        per_device,
        mesh=mesh,
        in_specs=(
            P("segment", "ctx", None),
            P("segment", None, None, None),
            P("segment", None, None),
            P("segment", None),
            P("segment", None, None),
            P("segment", None, None, None),
            P("segment", "ctx", None),
        ),
        out_specs=(
            P("segment", "ctx", None),
            P("segment", "ctx", None, None),
            P("segment", "ctx", None),
            P("segment", "ctx"),
            P("segment", "ctx", None),
            P("segment", "ctx", None, None),
            P("segment", "ctx", None),
        ),
        check_vma=False,
    )
```

```python
import functools

import jax
import jax.numpy as jnp
from jax import lax
from jax.experimental import pallas as pl
from jax.experimental.pallas import tpu as pltpu
from jax.sharding import PartitionSpec as P

MB = 16
REACH = 120.0
F32 = jnp.float32
BF16 = jnp.bfloat16
MESH = pl.DeviceIdType.MESH
NN = (((1,), (0,)), ((), ()))
NT = (((1,), (1,)), ((), ()))
TN = (((0,), (0,)), ((), ()))


def dot(left, right, dims):
    return lax.dot_general(left, right, dims, preferred_element_type=F32)


def split(value):
    high = value.astype(BF16)
    low = (value - high.astype(F32)).astype(BF16)
    return high, low


def cat(parts, axis):
    return jnp.concatenate(parts, axis=axis)


def stack(left, right, axis):
    return cat([left[0], right[0]], axis), cat([left[1], right[1]], axis)


def product(left, right, dims):
    left_axis, right_axis = dims[0][0][0], dims[0][1][0]
    left_both = cat(left, left_axis)
    wide = cat(right, 1 - right_axis)
    result = dot(left_both, cat([wide, wide], right_axis), dims)
    columns = result.shape[1] // 2
    return result[:, :columns] + result[:, columns:]


def row_mean(value):
    return jnp.mean(value, axis=-1, keepdims=True)


def fill_masks(ref, size):
    rows = lax.broadcasted_iota(jnp.int32, (size, size), 0)
    columns = lax.broadcasted_iota(jnp.int32, (size, size), 1)
    chosen = [rows >= columns, (rows // MB) > (columns // MB), rows == columns]
    block = MB
    while block < size:
        same = (rows // (2 * block)) == (columns // (2 * block))
        chosen.append(same & ((rows // block) > (columns // block)))
        block *= 2
    for index, mask in enumerate(chosen):
        ref[index] = jnp.where(mask, 1.0, 0.0).astype(F32)


def levels_of(size):
    levels, block = 0, MB
    while block < size:
        levels, block = levels + 1, 2 * block
    return levels


def together(streams):
    streams = list(streams)
    while streams:
        alive = []
        for stream in streams:
            try:
                next(stream)
                alive.append(stream)
            except StopIteration:
                pass
        streams = alive


def kernel(
    count, sections, heads, size, width,
    x_ref, og_ref, views_ref, gate_src, rate_src, gain_src, init_ref,
    next_ref, vgrad_ref, ggrad_ref, rgrad_ref, ngrad_ref, igrad_ref, prev_ref,
    gate_ref, rate_ref, gain_ref, view_buf, x_buf, og_buf, out_buf, dx_buf, masks,
    qs, ks, krs, qes, as_, ss, ts, fs, rs, dzs, ws, gs,
    kf, bs, sbs, os_, v0s, ls, ns, invs, sigs, rstds,
    init_buf, w_out0, w_out1, w_in0, w_in1, g_out0, g_out1, g_in0, g_in1, i_in0, i_in1,
    total, t_out0, t_out1, t_in0, t_in1, small, small_in,
    load_sem, own_sem, x_send, x_recv, og_send, og_recv, out_send, out_recv, dx_send, dx_recv,
    w_send, w_recv, g_send, g_recv, i_recv, t_send, t_recv, s_send, s_recv,
):
    me = lax.axis_index("ctx")
    section = lax.axis_index("segment")
    after = (section + 1) % sections
    before_me = (section + sections - 1) % sections
    chunks = count // 2
    late = me // chunks
    rank = me % chunks
    first = late * chunks
    partner = (me + chunks) % count
    lanes = 2 * heads

    def head_of(l, place):
        return ((1 - l // heads) * chunks + place) * heads + l % heads

    def columns(head):
        return pl.ds(pl.multiple_of(head * width, width), width)

    def mine(l):
        return head_of(l, rank)

    loads = []
    for block in range(2):
        start = mine(block * heads)
        here = pl.ds(block * heads, heads)
        loads.append(pltpu.make_async_copy(views_ref.at[0, pl.ds(start, heads)], view_buf.at[here], load_sem.at[block]))
        loads.append(pltpu.make_async_copy(init_ref.at[0, pl.ds(start, heads)], init_buf.at[here], load_sem.at[2 + block]))

    for index, (source, target) in enumerate(((gate_src, gate_ref), (rate_src, rate_ref), (gain_src, gain_ref))):
        loads.append(pltpu.make_async_copy(source, target, load_sem.at[4 + index]))

    def own(source, target, receive, l):
        return pltpu.make_async_copy(
            source.at[0, :, columns(mine(l))], target.at[l, rank], receive
        )

    barrier = pltpu.get_barrier_semaphore()
    for step in range(1, chunks):
        pl.semaphore_signal(
            barrier, inc=1, device_id=(section, first + (rank + step) % chunks), device_id_type=MESH
        )
    pl.semaphore_signal(barrier, inc=1, device_id=(section, partner), device_id_type=MESH)
    for c in range(chunks):
        pl.semaphore_signal(barrier, inc=1, device_id=(after, first + c), device_id_type=MESH)
        pl.semaphore_signal(barrier, inc=1, device_id=(before_me, first + c), device_id_type=MESH)
    for load in loads:
        load.start()
    for l in range(lanes):
        own(x_ref, x_buf, own_sem.at[0], l).start()
        own(og_ref, og_buf, own_sem.at[1], l).start()

    def remote(source, target, send, receive, device):
        return pltpu.make_async_remote_copy(
            src_ref=source, dst_ref=target, send_sem=send, recv_sem=receive,
            device_id=device, device_id_type=MESH,
        )

    def settle(ref, semaphore):
        pltpu.make_async_copy(ref, ref, semaphore).wait()

    def spread(source, target, send, receive, l):
        for step in range(1, chunks):
            peer = (rank + step) % chunks
            remote(
                source.at[0, :, columns(head_of(l, peer))], target.at[l, rank],
                send.at[0], receive.at[l], (section, first + peer),
            ).start()

    def collect(source, target, send, receive, l, c, to):
        remote(
            source.at[l, c], target.at[0, :, columns(mine(l))],
            send.at[0], receive.at[0], (to, first + c),
        ).start()

    pl.semaphore_wait(barrier, 3 * chunks)
    for l in range(lanes):
        spread(x_ref, x_buf, x_send, x_recv, l)
    for load in loads:
        load.wait()
    scale = 1.0 / (MB * width)
    levels = levels_of(size)
    fill_masks(masks, size)

    def gate_of(l):
        return gate_ref[0, pl.ds(mine(l), 1), :]

    def gain_of(l):
        return gain_ref[0, pl.ds(mine(l), 1), :]

    def base_of(l):
        lane = lax.broadcasted_iota(jnp.int32, rate_ref.shape, 1)
        return jnp.sum(jnp.where(lane == mine(l), rate_ref[...], 0.0), axis=1, keepdims=True)

    def put(ref, l, c, pair):
        ref[l, c, 0] = pair[0]
        ref[l, c, 1] = pair[1]

    def get(ref, l, c):
        return ref[l, c, 0], ref[l, c, 1]

    def prepare(l, c):
        x = x_buf[l, c]
        packed = dot(x, view_buf[l], NN)
        yield
        q = packed[:, :width]
        raw = packed[:, width : 2 * width]
        inv = lax.rsqrt(row_mean(raw * raw) + 1e-06)
        k = raw * inv
        y = packed[:, 2 * width :] - k
        logit = jnp.sum(x.astype(F32) * gate_of(l), axis=-1, keepdims=True)
        sig = jax.nn.sigmoid(logit)
        kr = k * (base_of(l) * sig * scale)
        k2, q2, kr2 = split(k), split(q), split(kr)
        y2 = split(y)
        yield
        grams = product(stack(k2, q2, 0), kr2, NT)
        yield
        scores = split(masks[0] * grams[size:])
        strict = grams[:size]
        inverse = masks[2] - masks[3] * strict if levels else masks[2]
        t2 = split(inverse)
        for level in range(1, levels):
            half_way = product(t2, split(masks[3 + level] * strict), NN)
            yield
            inverse = inverse - product(split(half_way), t2, NN)
            t2 = split(inverse)
            yield
        ab = product(t2, stack(k2, y2, 1), NN)
        yield
        ab2 = split(ab)
        sab = product(scores, ab2, NN)
        fo = product(kr2, ab2, TN)
        yield
        put(qs, l, c, q2)
        put(ks, l, c, k2)
        put(krs, l, c, kr2)
        put(qes, l, c, split(q - sab[:, :width]))
        put(as_, l, c, (ab2[0][:, :width], ab2[1][:, :width]))
        put(ss, l, c, scores)
        put(ts, l, c, t2)
        put(fs, l, c, split(fo[:, :width]))
        kf[l, c] = k
        bs[l, c] = ab[:, width:]
        sbs[l, c] = sab[:, width:]
        os_[l, c] = fo[:, width:]
        invs[l, c] = inv
        sigs[l, c] = sig

    def emit(l, c):
        moved = product(stack(get(qes, l, c), get(as_, l, c), 0), get(ws, l, c), NN)
        yield
        z = moved[:size] + sbs[l, c]
        put(rs, l, c, split(moved[size:] - bs[l, c]))
        centred = z - row_mean(z)
        yield
        rstd = lax.rsqrt(row_mean(centred * centred) + 1e-05)
        normed = centred * rstd
        out_buf[l, c] = (x_buf[l, c].astype(F32) + gain_of(l) * normed).astype(BF16)
        ns[l, c] = normed
        rstds[l, c] = rstd
        yield

    def receive_grad(l, c, gains):
        dout = og_buf[l, c].astype(F32)
        normed = ns[l, c]
        gains.append(jnp.sum(dout * normed, axis=0, keepdims=True))
        dn = dout * gain_of(l)
        dz = rstds[l, c] * (dn - row_mean(dn) - normed * row_mean(dn * normed))
        dz2 = split(dz)
        put(dzs, l, c, dz2)
        yield
        back = product(stack(get(qes, l, c), get(ss, l, c), 1), dz2, TN)
        ls[l, c] = back[:width]
        v0s[l, c] = back[width:]
        yield

    def gradients(l, c, found):
        g2 = get(gs, l, c)
        kr2, w2, r2, dz2 = get(krs, l, c), get(ws, l, c), get(rs, l, c), get(dzs, l, c)
        v = v0s[l, c] + product(kr2, g2, NN)
        yield
        du = -product(get(ts, l, c), split(v), TN)
        yield
        both = stack(dz2, split(du), 0)
        inner = product(both, r2, NT)
        yield
        d2 = stack(split(-masks[0] * inner[:size]), split(-masks[1] * inner[size:]), 0)
        dqk = product(both, w2, NT) + product(d2, kr2, NN)
        yield
        dkr = product(d2, stack(get(qs, l, c), get(ks, l, c), 0), TN) - product(r2, g2, NT)
        yield
        sig, inv, k, base = sigs[l, c], invs[l, c], kf[l, c], base_of(l)
        rate_factor = sig * scale
        dk = dqk[size:] + (base * rate_factor) * dkr + du
        draw = inv * (dk - k * row_mean(dk * k))
        drate = jnp.sum(dkr * k, axis=-1, keepdims=True) * rate_factor
        dlogit = drate * base * (1.0 - sig)
        found.append((
            jnp.sum(dlogit * x_buf[l, c].astype(F32), axis=0, keepdims=True),
            jnp.sum(drate, axis=0, keepdims=True),
            split(cat([dqk[:size], draw, -du], 1)),
            dlogit,
        ))

    every = range(chunks)
    batches = [range(start, min(start + 4, chunks)) for start in range(0, chunks, 4)]

    def encode(value, coded, peaks):
        peak = jnp.max(jnp.abs(value), axis=0, keepdims=True) + 1e-30
        level = jnp.exp2(jnp.abs(value) * (2 * REACH / peak) - REACH)
        coded[...] = jnp.where(value < 0, -level, level).astype(BF16)
        peaks[...] = peak

    def decode(coded, peaks):
        value = coded[...].astype(F32)
        level = (jnp.log2(jnp.abs(value)) + REACH) * (peaks[...] * (0.5 / REACH))
        return jnp.where(value < 0, -level, level)

    def across(source, target, i, k, send, receive):
        return [
            remote(source[part].at[i], target[part].at[k], send.at[part], receive.at[part, k], (section, partner))
            for part in range(2)
        ]

    def send_across(*details):
        for copy in across(*details):
            copy.start()

    def landed(target, k, receive):
        for part in range(2):
            settle(target[part].at[k], receive.at[part, k])

    def refs_of(pair, l):
        return pair[0].at[l], pair[1].at[l]

    w_out, w_in, g_out, g_in = (w_out0, w_out1), (w_in0, w_in1), (g_out0, g_out1), (g_in0, g_in1)
    i_in, total_out, total_in = (i_in0, i_in1), (t_out0, t_out1), (t_in0, t_in1)

    def later(steps, stream):
        for _ in range(steps):
            yield
        yield from stream

    def advance(l, held, last):
        for c in every:
            pair = split(held)
            put(ws, l, c, pair)
            if c < chunks - 1 or last:
                moved = product(get(fs, l, c), pair, NN)
                yield
                held = held - moved + os_[l, c]
        if last:
            encode(held, *refs_of(w_out, l))
            send_across(w_out, w_in, l, l, w_send, w_recv)

    def retreat(l, held, done):
        for c in reversed(every):
            if held is None:
                zero = jnp.zeros((width, width), BF16)
                put(gs, l, c, (zero, zero))
                held = ls[l, c]
                continue
            pair = split(held)
            put(gs, l, c, pair)
            moved = product(get(fs, l, c), pair, TN)
            yield
            held = held - moved + ls[l, c]
        done(held)

    small[...] = jnp.zeros_like(small)
    settle(x_buf.at[:, 0], own_sem.at[0])
    together(prepare(l, rank) for l in range(lanes))

    def prepare_rest(l):
        settle(x_buf.at[l, pl.ds(0, chunks - 1)], x_recv.at[l])
        return [prepare(l, (rank + 1 + c) % chunks) for c in range(chunks - 1)]

    def outputs(l):
        for c in every:
            collect(out_buf, next_ref, out_send, out_recv, l, c, after)

    def ahead(l):
        return [advance(l, init_buf[l], True)] + [later(c + 1, emit(l, c)) for c in every]

    def received(l, gains):
        settle(og_buf.at[l, pl.ds(0, chunks - 1)], og_recv.at[l])
        return [receive_grad(l, c, gains) for c in every]

    def keep_gains(l, gains):
        small[l, 1:2, :] = sum(gains)

    def keep_start(l):
        slot = l % heads

        def done(held):
            igrad_ref[0, slot] = held
            encode(held, *refs_of(g_out, l))

        return done

    def send_start(l):
        @pl.when(l < heads)
        def _():
            send_across(g_out, i_in, l, l % heads, g_send, i_recv)

    def find_gradients(l, beside=()):
        slot = l % heads
        found = []
        for batch in batches:
            some = []
            together([gradients(l, c, some) for c in batch] + list(beside))
            beside = ()
            found += some
            views = cat([view_buf[l]] * 2, 1)
            wide = cat([cat(item[2], 1) for item in some], 0)
            dx = dot(wide, views, NT)
            for index, c in enumerate(batch):
                part = dx[index * size : (index + 1) * size]
                part = part + og_buf[l, c].astype(F32) + some[index][3] * gate_of(l)
                dx_buf[l, c] = part.astype(BF16)
            for c in batch:
                collect(dx_buf, prev_ref, dx_send, dx_recv, l, c, before_me)
        small[l, 0:1, :] = sum(item[0] for item in found)
        small[l, 2:3, :] = jnp.broadcast_to(sum(item[1] for item in found), (1, width))
        tokens = cat([x_buf[l, c] for c in every for _ in range(2)], 0)
        whole = dot(tokens, cat([half for item in found for half in item[2]], 0), TN)
        foreign = (l // heads) == late

        @pl.when(foreign)
        def _():
            encode(whole, *refs_of(total_out, slot))
            send_across(total_out, total_in, slot, slot, t_send, t_recv)
            remote(small.at[l], small_in.at[slot], s_send.at[0], s_recv.at[slot], (section, partner)).start()

        @pl.when(jnp.logical_not(foreign))
        def _():
            total[slot] = whole

    @pl.when(late == 0)
    def _():
        together(prepare_rest(0))
        spread(og_ref, og_buf, og_send, og_recv, 0)

        def first_step(l, carry):
            together(prepare_rest(l) + ahead(l - 1))
            outputs(l - 1)
            spread(og_ref, og_buf, og_send, og_recv, l)
            return carry

        lax.fori_loop(1, lanes, first_step, 0)
        together(ahead(lanes - 1))
        outputs(lanes - 1)
        settle(og_buf.at[:, 0], own_sem.at[1])

        gains = []
        together(received(0, gains))
        keep_gains(0, gains)
        landed(g_in, 0, g_recv)
        together([retreat(0, decode(*refs_of(g_in, 0)), keep_start(0))])
        send_start(0)

        def second_step(l, carry):
            gains = []
            landed(g_in, l, g_recv)
            streams = received(l, gains)
            streams.append(later(3, retreat(l, decode(*refs_of(g_in, l)), keep_start(l))))
            find_gradients(l - 1, streams)
            keep_gains(l, gains)
            send_start(l)
            return carry

        lax.fori_loop(1, lanes, second_step, 0)

    @pl.when(late == 1)
    def _():
        def first_step(l, carry):
            together(prepare_rest(l))
            spread(og_ref, og_buf, og_send, og_recv, l)
            return carry

        lax.fori_loop(0, lanes, first_step, 0)
        settle(og_buf.at[:, 0], own_sem.at[1])

        def second_step(l, carry):
            landed(w_in, l, w_recv)
            together(
                [advance(l, decode(*refs_of(w_in, l)), False)]
                + [later(c + 1, emit(l, c)) for c in every]
            )
            outputs(l)
            gains = []
            together(received(l, gains))
            keep_gains(l, gains)

            def done(held):
                encode(held, *refs_of(g_out, l))
                send_across(g_out, g_in, l, l, g_send, g_recv)

            together([retreat(l, None, done)])
            return carry

        lax.fori_loop(0, lanes, second_step, 0)

    def third_step(step, carry):
        find_gradients(jnp.where(late == 0, lanes - 1, (step + heads) % lanes))
        return carry

    lax.fori_loop(0, jnp.where(late == 0, 1, lanes), third_step, 0)

    for h in range(heads):
        landed(total_in, h, t_recv)
        settle(small_in.at[h], s_recv.at[h])
        vgrad_ref[0, h] = total[h] + decode(*refs_of(total_in, h))
        sums = small[(1 - late) * heads + h] + small_in[h]
        ggrad_ref[0, h : h + 1, :] = sums[0:1]
        ngrad_ref[0, h : h + 1, :] = sums[1:2]
        rgrad_ref[:, h : h + 1] = sums[2:3, 0:1]

    @pl.when(late == 1)
    def _():
        for h in range(heads):
            landed(i_in, h, i_recv)
            igrad_ref[0, h] = decode(*refs_of(i_in, h))

    settle(x_buf.at[:, pl.ds(0, chunks - 1)], x_send.at[0])
    settle(og_buf.at[:, pl.ds(0, chunks - 1)], og_send.at[0])
    settle(small_in, s_send.at[0])
    for part in range(2):
        settle(total_out[part], t_send.at[part])

    @pl.when(late == 0)
    def _():
        for part in range(2):
            settle(w_out[part], w_send.at[part])
            settle(i_in[part], g_send.at[part])

    @pl.when(late == 1)
    def _():
        for part in range(2):
            settle(g_out[part], g_send.at[part])

    settle(out_buf, out_send.at[0])
    settle(dx_buf, dx_send.at[0])
    settle(next_ref, out_recv.at[0])
    settle(prev_ref, dx_recv.at[0])


def hand_over(*refs):
    number = (len(refs) - 1) // 2
    copies = [pltpu.make_async_copy(refs[i], refs[number + i], refs[-1].at[i]) for i in range(number)]
    for copy in copies:
        copy.start()
    for copy in copies:
        copy.wait()


def per_device(segment_input, views, gate_vec, base_rate, norm_gain, init_weight, out_grad):
    count = lax.axis_size("ctx")
    size, features = segment_input.shape[1:]
    every, width = gate_vec.shape[1:]
    heads = every // count
    lanes, chunks = 2 * heads, count // 2

    def shaped(shape, kind):
        return jax.ShapeDtypeStruct(shape, kind)

    vmem = pl.BlockSpec(memory_space=pltpu.VMEM)
    hbm = pl.BlockSpec(memory_space=pltpu.HBM)

    def pairs(rows, columns):
        return pltpu.VMEM((lanes, chunks, 2, rows, columns), BF16)

    def floats(rows, columns):
        return pltpu.VMEM((lanes, chunks, rows, columns), F32)

    tokens = pltpu.VMEM((lanes, chunks, size, width), BF16)
    matrix = pltpu.VMEM((lanes, width, width), F32)
    semaphores = [
        (7,), (2,), (1,), (lanes,), (1,), (lanes,), (1,), (1,), (1,), (1,),
        (2,), (2, lanes), (2,), (2, lanes), (2, heads), (2,), (2, heads), (1,), (heads,),
    ]
    def coded(number, columns):
        return pltpu.VMEM((number, width, columns), BF16), pltpu.VMEM((number, 1, columns), F32)

    results = pl.pallas_call(
        functools.partial(kernel, count, lax.axis_size("segment"), heads, size, width),
        out_shape=(
            pltpu.VMEM((1, size, features), BF16),
            pltpu.VMEM((1, heads, width, 3 * width), F32),
            pltpu.VMEM((1, heads, width), F32),
            pltpu.VMEM((1, heads), F32),
            pltpu.VMEM((1, heads, width), F32),
            pltpu.VMEM((1, heads, width, width), F32),
            pltpu.VMEM((1, size, features), BF16),
        ),
        in_specs=[hbm] * 7,
        out_specs=(vmem,) * 7,
        scratch_shapes=[
            pltpu.VMEM(gate_vec.shape, F32),
            pltpu.VMEM(base_rate.shape, F32),
            pltpu.VMEM(norm_gain.shape, F32),
            pltpu.VMEM((lanes, width, 3 * width), BF16),
            tokens, tokens, tokens, tokens,
            pltpu.VMEM((3 + levels_of(size), size, size), F32),
            pairs(size, width), pairs(size, width), pairs(size, width), pairs(size, width), pairs(size, width),
            pairs(size, size), pairs(size, size), pairs(width, width),
            pairs(size, width), pairs(size, width), pairs(width, width), pairs(width, width),
            floats(size, width), floats(size, width), floats(size, width), floats(width, width),
            floats(size, width), floats(width, width), floats(size, width),
            floats(size, 1), floats(size, 1), floats(size, 1),
            matrix,
            *coded(lanes, width), *coded(lanes, width), *coded(lanes, width), *coded(lanes, width),
            *coded(heads, width),
            pltpu.VMEM((heads, width, 3 * width), F32),
            *coded(heads, 3 * width), *coded(heads, 3 * width),
            pltpu.VMEM((lanes, 8, width), F32),
            pltpu.VMEM((heads, 8, width), F32),
            *[pltpu.SemaphoreType.DMA(numbers) for numbers in semaphores],
        ],
        compiler_params=pltpu.CompilerParams(
            vmem_limit_bytes=52 * 1024 * 1024, collective_id=0, has_side_effects=True
        ),
    )(*[
        pltpu.with_memory_space_constraint(value, pltpu.HBM)
        for value in (segment_input, out_grad, views, gate_vec, base_rate, norm_gain, init_weight)
    ])
    results = [pltpu.with_memory_space_constraint(value, pltpu.VMEM) for value in results]
    return pl.pallas_call(
        hand_over,
        out_shape=tuple(shaped(value.shape, value.dtype) for value in results),
        in_specs=[vmem] * len(results),
        out_specs=(hbm,) * len(results),
        scratch_shapes=[pltpu.SemaphoreType.DMA((len(results),))],
    )(*results)


def solution(mesh):
    return jax.shard_map(
        per_device,
        mesh=mesh,
        in_specs=(
            P("segment", "ctx", None),
            P("segment", None, None, None),
            P("segment", None, None),
            P("segment", None),
            P("segment", None, None),
            P("segment", None, None, None),
            P("segment", "ctx", None),
        ),
        out_specs=(
            P("segment", "ctx", None),
            P("segment", "ctx", None, None),
            P("segment", "ctx", None),
            P("segment", "ctx"),
            P("segment", "ctx", None),
            P("segment", "ctx", None, None),
            P("segment", "ctx", None),
        ),
        check_vma=False,
    )
```

```python
import functools

import jax
import jax.numpy as jnp
from jax import lax
from jax.experimental import pallas as pl
from jax.experimental.pallas import tpu as pltpu
from jax.sharding import PartitionSpec as P

MB = 16
REACH = 120.0
F32 = jnp.float32
BF16 = jnp.bfloat16
MESH = pl.DeviceIdType.MESH
NN = (((1,), (0,)), ((), ()))
NT = (((1,), (1,)), ((), ()))
TN = (((0,), (0,)), ((), ()))


def dot(left, right, dims):
    return lax.dot_general(left, right, dims, preferred_element_type=F32)


def split(value):
    high = value.astype(BF16)
    low = (value - high.astype(F32)).astype(BF16)
    return high, low


def cat(parts, axis):
    return jnp.concatenate(parts, axis=axis)


def stack(left, right, axis):
    return cat([left[0], right[0]], axis), cat([left[1], right[1]], axis)


def product(left, right, dims):
    left_axis, right_axis = dims[0][0][0], dims[0][1][0]
    left_both = cat(left, left_axis)
    wide = cat(right, 1 - right_axis)
    result = dot(left_both, cat([wide, wide], right_axis), dims)
    columns = result.shape[1] // 2
    return result[:, :columns] + result[:, columns:]


def row_mean(value):
    return jnp.mean(value, axis=-1, keepdims=True)


def fill_masks(ref, size):
    rows = lax.broadcasted_iota(jnp.int32, (size, size), 0)
    columns = lax.broadcasted_iota(jnp.int32, (size, size), 1)
    chosen = [rows >= columns, (rows // MB) > (columns // MB), rows == columns]
    block = MB
    while block < size:
        same = (rows // (2 * block)) == (columns // (2 * block))
        chosen.append(same & ((rows // block) > (columns // block)))
        block *= 2
    for index, mask in enumerate(chosen):
        ref[index] = jnp.where(mask, 1.0, 0.0).astype(F32)


def levels_of(size):
    levels, block = 0, MB
    while block < size:
        levels, block = levels + 1, 2 * block
    return levels


def together(streams):
    streams = list(streams)
    while streams:
        alive = []
        for stream in streams:
            try:
                next(stream)
                alive.append(stream)
            except StopIteration:
                pass
        streams = alive


def kernel(
    count, sections, heads, size, width,
    x_ref, og_ref, views_ref, gate_src, rate_src, gain_src, init_ref,
    next_ref, vgrad_ref, ggrad_ref, rgrad_ref, ngrad_ref, igrad_ref, prev_ref,
    gate_ref, rate_ref, gain_ref, view_buf, x_buf, og_buf, out_buf, dx_buf, masks,
    qs, ks, krs, qes, as_, ss, ts, fs, rs, dzs, ws, gs,
    kf, bs, sbs, os_, v0s, ls, ns, invs, sigs, rstds,
    init_buf, w_out0, w_out1, w_in0, w_in1, g_out0, g_out1, g_in0, g_in1, i_in0, i_in1,
    total, t_out0, t_out1, t_in0, t_in1, small, small_in,
    load_sem, own_sem, x_send, x_recv, og_send, og_recv, out_send, out_recv, dx_send, dx_recv,
    w_send, w_recv, g_send, g_recv, i_recv, t_send, t_recv, s_send, s_recv,
):
    me = lax.axis_index("ctx")
    section = lax.axis_index("segment")
    after = (section + 1) % sections
    before_me = (section + sections - 1) % sections
    chunks = count // 2
    late = me // chunks
    rank = me % chunks
    first = late * chunks
    partner = (me + chunks) % count
    lanes = 2 * heads

    def head_of(l, place):
        return ((1 - l // heads) * chunks + place) * heads + l % heads

    def columns(head):
        return pl.ds(pl.multiple_of(head * width, width), width)

    def mine(l):
        return head_of(l, rank)

    loads = []
    for block in range(2):
        start = mine(block * heads)
        here = pl.ds(block * heads, heads)
        loads.append(pltpu.make_async_copy(views_ref.at[0, pl.ds(start, heads)], view_buf.at[here], load_sem.at[block]))
        loads.append(pltpu.make_async_copy(init_ref.at[0, pl.ds(start, heads)], init_buf.at[here], load_sem.at[2 + block]))

    for index, (source, target) in enumerate(((gate_src, gate_ref), (rate_src, rate_ref), (gain_src, gain_ref))):
        loads.append(pltpu.make_async_copy(source, target, load_sem.at[4 + index]))

    def own(source, target, receive, l):
        return pltpu.make_async_copy(
            source.at[0, :, columns(mine(l))], target.at[l, rank], receive
        )

    barrier = pltpu.get_barrier_semaphore()
    for step in range(1, chunks):
        pl.semaphore_signal(
            barrier, inc=1, device_id=(section, first + (rank + step) % chunks), device_id_type=MESH
        )
    pl.semaphore_signal(barrier, inc=1, device_id=(section, partner), device_id_type=MESH)
    for c in range(chunks):
        pl.semaphore_signal(barrier, inc=1, device_id=(after, first + c), device_id_type=MESH)
        pl.semaphore_signal(barrier, inc=1, device_id=(before_me, first + c), device_id_type=MESH)
    for load in loads:
        load.start()
    for l in range(lanes):
        own(x_ref, x_buf, own_sem.at[0], l).start()
        own(og_ref, og_buf, own_sem.at[1], l).start()

    def remote(source, target, send, receive, device):
        return pltpu.make_async_remote_copy(
            src_ref=source, dst_ref=target, send_sem=send, recv_sem=receive,
            device_id=device, device_id_type=MESH,
        )

    def settle(ref, semaphore):
        pltpu.make_async_copy(ref, ref, semaphore).wait()

    def spread(source, target, send, receive, l):
        for step in range(1, chunks):
            peer = (rank + step) % chunks
            remote(
                source.at[0, :, columns(head_of(l, peer))], target.at[l, rank],
                send.at[0], receive.at[l], (section, first + peer),
            ).start()

    def collect(source, target, send, receive, l, c, to):
        remote(
            source.at[l, c], target.at[0, :, columns(mine(l))],
            send.at[0], receive.at[0], (to, first + c),
        ).start()

    pl.semaphore_wait(barrier, 3 * chunks)
    for l in range(lanes):
        spread(x_ref, x_buf, x_send, x_recv, l)
    for load in loads:
        load.wait()
    scale = 1.0 / (MB * width)
    levels = levels_of(size)
    fill_masks(masks, size)

    def gate_of(l):
        return gate_ref[0, pl.ds(mine(l), 1), :]

    def gain_of(l):
        return gain_ref[0, pl.ds(mine(l), 1), :]

    def base_of(l):
        lane = lax.broadcasted_iota(jnp.int32, rate_ref.shape, 1)
        return jnp.sum(jnp.where(lane == mine(l), rate_ref[...], 0.0), axis=1, keepdims=True)

    def put(ref, l, c, pair):
        ref[l, c, 0] = pair[0]
        ref[l, c, 1] = pair[1]

    def get(ref, l, c):
        return ref[l, c, 0], ref[l, c, 1]

    def prepare(l, c, packed=None):
        x = x_buf[l, c]
        if packed is None:
            packed = dot(x, view_buf[l], NN)
            yield
        q = packed[:, :width]
        raw = packed[:, width : 2 * width]
        inv = lax.rsqrt(row_mean(raw * raw) + 1e-06)
        k = raw * inv
        y = packed[:, 2 * width :] - k
        logit = jnp.sum(x.astype(F32) * gate_of(l), axis=-1, keepdims=True)
        sig = jax.nn.sigmoid(logit)
        kr = k * (base_of(l) * sig * scale)
        k2, q2, kr2 = split(k), split(q), split(kr)
        y2 = split(y)
        yield
        grams = product(stack(k2, q2, 0), kr2, NT)
        yield
        scores = split(masks[0] * grams[size:])
        strict = grams[:size]
        inverse = masks[2] - masks[3] * strict if levels else masks[2]
        t2 = split(inverse)
        for level in range(1, levels):
            half_way = product(t2, split(masks[3 + level] * strict), NN)
            yield
            inverse = inverse - product(split(half_way), t2, NN)
            t2 = split(inverse)
            yield
        ab = product(t2, stack(k2, y2, 1), NN)
        yield
        ab2 = split(ab)
        sab = product(scores, ab2, NN)
        fo = product(kr2, ab2, TN)
        yield
        put(qs, l, c, q2)
        put(ks, l, c, k2)
        put(krs, l, c, kr2)
        put(qes, l, c, split(q - sab[:, :width]))
        put(as_, l, c, (ab2[0][:, :width], ab2[1][:, :width]))
        put(ss, l, c, scores)
        put(ts, l, c, t2)
        put(fs, l, c, split(fo[:, :width]))
        kf[l, c] = k
        bs[l, c] = ab[:, width:]
        sbs[l, c] = sab[:, width:]
        os_[l, c] = fo[:, width:]
        invs[l, c] = inv
        sigs[l, c] = sig

    def emit(l, c):
        moved = product(stack(get(qes, l, c), get(as_, l, c), 0), get(ws, l, c), NN)
        yield
        z = moved[:size] + sbs[l, c]
        put(rs, l, c, split(moved[size:] - bs[l, c]))
        centred = z - row_mean(z)
        yield
        rstd = lax.rsqrt(row_mean(centred * centred) + 1e-05)
        normed = centred * rstd
        out_buf[l, c] = (x_buf[l, c].astype(F32) + gain_of(l) * normed).astype(BF16)
        ns[l, c] = normed
        rstds[l, c] = rstd
        yield

    def receive_grad(l, c, gains):
        dout = og_buf[l, c].astype(F32)
        normed = ns[l, c]
        gains.append(jnp.sum(dout * normed, axis=0, keepdims=True))
        dn = dout * gain_of(l)
        dz = rstds[l, c] * (dn - row_mean(dn) - normed * row_mean(dn * normed))
        dz2 = split(dz)
        put(dzs, l, c, dz2)
        yield
        back = product(stack(get(qes, l, c), get(ss, l, c), 1), dz2, TN)
        ls[l, c] = back[:width]
        v0s[l, c] = back[width:]
        yield

    def gradients(l, c, found):
        g2 = get(gs, l, c)
        kr2, w2, r2, dz2 = get(krs, l, c), get(ws, l, c), get(rs, l, c), get(dzs, l, c)
        v = v0s[l, c] + product(kr2, g2, NN)
        yield
        du = -product(get(ts, l, c), split(v), TN)
        yield
        both = stack(dz2, split(du), 0)
        inner = product(both, r2, NT)
        yield
        d2 = stack(split(-masks[0] * inner[:size]), split(-masks[1] * inner[size:]), 0)
        dqk = product(both, w2, NT) + product(d2, kr2, NN)
        yield
        dkr = product(d2, stack(get(qs, l, c), get(ks, l, c), 0), TN) - product(r2, g2, NT)
        yield
        sig, inv, k, base = sigs[l, c], invs[l, c], kf[l, c], base_of(l)
        rate_factor = sig * scale
        dk = dqk[size:] + (base * rate_factor) * dkr + du
        draw = inv * (dk - k * row_mean(dk * k))
        drate = jnp.sum(dkr * k, axis=-1, keepdims=True) * rate_factor
        dlogit = drate * base * (1.0 - sig)
        found.append((
            jnp.sum(dlogit * x_buf[l, c].astype(F32), axis=0, keepdims=True),
            jnp.sum(drate, axis=0, keepdims=True),
            split(cat([dqk[:size], draw, -du], 1)),
            dlogit,
        ))

    every = range(chunks)
    batches = [range(start, min(start + 4, chunks)) for start in range(0, chunks, 4)]

    def encode(value, coded, peaks):
        peak = jnp.max(jnp.abs(value), axis=0, keepdims=True) + 1e-30
        level = jnp.exp2(jnp.abs(value) * (2 * REACH / peak) - REACH)
        coded[...] = jnp.where(value < 0, -level, level).astype(BF16)
        peaks[...] = peak

    def decode(coded, peaks):
        value = coded[...].astype(F32)
        level = (jnp.log2(jnp.abs(value)) + REACH) * (peaks[...] * (0.5 / REACH))
        return jnp.where(value < 0, -level, level)

    def across(source, target, i, k, send, receive):
        return [
            remote(source[part].at[i], target[part].at[k], send.at[part], receive.at[part, k], (section, partner))
            for part in range(2)
        ]

    def send_across(*details):
        for copy in across(*details):
            copy.start()

    def landed(target, k, receive):
        for part in range(2):
            settle(target[part].at[k], receive.at[part, k])

    def refs_of(pair, l):
        return pair[0].at[l], pair[1].at[l]

    w_out, w_in, g_out, g_in = (w_out0, w_out1), (w_in0, w_in1), (g_out0, g_out1), (g_in0, g_in1)
    i_in, total_out, total_in = (i_in0, i_in1), (t_out0, t_out1), (t_in0, t_in1)

    def later(steps, stream):
        for _ in range(steps):
            yield
        yield from stream

    def advance(l, held, last):
        for c in every:
            pair = split(held)
            put(ws, l, c, pair)
            if c < chunks - 1 or last:
                moved = product(get(fs, l, c), pair, NN)
                yield
                held = held - moved + os_[l, c]
        if last:
            encode(held, *refs_of(w_out, l))
            send_across(w_out, w_in, l, l, w_send, w_recv)

    def retreat(l, held, done):
        for c in reversed(every):
            if held is None:
                zero = jnp.zeros((width, width), BF16)
                put(gs, l, c, (zero, zero))
                held = ls[l, c]
                continue
            pair = split(held)
            put(gs, l, c, pair)
            moved = product(get(fs, l, c), pair, TN)
            yield
            held = held - moved + ls[l, c]
        done(held)

    small[...] = jnp.zeros_like(small)
    settle(x_buf.at[:, 0], own_sem.at[0])
    together(prepare(l, rank) for l in range(lanes))

    def prepare_rest(l):
        settle(x_buf.at[l, pl.ds(0, chunks - 1)], x_recv.at[l])
        places = [(rank + 1 + c) % chunks for c in range(chunks - 1)]
        packed = dot(cat([x_buf[l, c] for c in places], 0), view_buf[l], NN)
        return [prepare(l, c, packed[i * size : (i + 1) * size]) for i, c in enumerate(places)]

    def outputs(l):
        for c in every:
            collect(out_buf, next_ref, out_send, out_recv, l, c, after)

    def ahead(l):
        return [advance(l, init_buf[l], True)] + [later(c + 1, emit(l, c)) for c in every]

    def received(l, gains):
        settle(og_buf.at[l, pl.ds(0, chunks - 1)], og_recv.at[l])
        return [receive_grad(l, c, gains) for c in every]

    def keep_gains(l, gains):
        small[l, 1:2, :] = sum(gains)

    def keep_start(l):
        slot = l % heads

        def done(held):
            igrad_ref[0, slot] = held

        return done

    def send_start(l):
        @pl.when(l < heads)
        def _():
            encode(igrad_ref[0, l % heads], *refs_of(g_out, l))
            send_across(g_out, i_in, l, l % heads, g_send, i_recv)

    def find_gradients(l, beside=()):
        slot = l % heads
        found = []
        for batch in batches:
            some = []
            together([gradients(l, c, some) for c in batch] + list(beside))
            beside = ()
            found += some
            views = cat([view_buf[l]] * 2, 1)
            wide = cat([cat(item[2], 1) for item in some], 0)
            dx = dot(wide, views, NT)
            for index, c in enumerate(batch):
                part = dx[index * size : (index + 1) * size]
                part = part + og_buf[l, c].astype(F32) + some[index][3] * gate_of(l)
                dx_buf[l, c] = part.astype(BF16)
            for c in batch:
                collect(dx_buf, prev_ref, dx_send, dx_recv, l, c, before_me)
        small[l, 0:1, :] = sum(item[0] for item in found)
        small[l, 2:3, :] = jnp.broadcast_to(sum(item[1] for item in found), (1, width))
        tokens = cat([x_buf[l, c] for c in every for _ in range(2)], 0)
        whole = dot(tokens, cat([half for item in found for half in item[2]], 0), TN)
        foreign = (l // heads) == late

        @pl.when(foreign)
        def _():
            encode(whole, *refs_of(total_out, slot))
            send_across(total_out, total_in, slot, slot, t_send, t_recv)
            remote(small.at[l], small_in.at[slot], s_send.at[0], s_recv.at[slot], (section, partner)).start()

        @pl.when(jnp.logical_not(foreign))
        def _():
            total[slot] = whole

    @pl.when(late == 0)
    def _():
        together(prepare_rest(0))
        spread(og_ref, og_buf, og_send, og_recv, 0)

        def first_step(l, carry):
            together(prepare_rest(l) + ahead(l - 1))
            outputs(l - 1)
            spread(og_ref, og_buf, og_send, og_recv, l)
            return carry

        lax.fori_loop(1, lanes, first_step, 0)
        together(ahead(lanes - 1))
        outputs(lanes - 1)
        settle(og_buf.at[:, 0], own_sem.at[1])

        gains = []
        together(received(0, gains))
        keep_gains(0, gains)
        landed(g_in, 0, g_recv)
        together([retreat(0, decode(*refs_of(g_in, 0)), keep_start(0))])
        send_start(0)

        def second_step(l, carry):
            gains = []
            landed(g_in, l, g_recv)
            streams = received(l, gains)
            streams.append(later(3, retreat(l, decode(*refs_of(g_in, l)), keep_start(l))))
            find_gradients(l - 1, streams)
            keep_gains(l, gains)
            send_start(l)
            return carry

        lax.fori_loop(1, lanes, second_step, 0)

    @pl.when(late == 1)
    def _():
        def first_step(l, carry):
            together(prepare_rest(l))
            spread(og_ref, og_buf, og_send, og_recv, l)
            return carry

        lax.fori_loop(0, lanes, first_step, 0)
        settle(og_buf.at[:, 0], own_sem.at[1])

        def second_step(l, carry):
            landed(w_in, l, w_recv)
            together(
                [advance(l, decode(*refs_of(w_in, l)), False)]
                + [later(c + 1, emit(l, c)) for c in every]
            )
            outputs(l)
            gains = []
            together(received(l, gains))
            keep_gains(l, gains)

            def done(held):
                encode(held, *refs_of(g_out, l))
                send_across(g_out, g_in, l, l, g_send, g_recv)

            together([retreat(l, None, done)])
            return carry

        lax.fori_loop(0, lanes, second_step, 0)

    def third_step(step, carry):
        find_gradients(jnp.where(late == 0, lanes - 1, (step + heads) % lanes))
        return carry

    lax.fori_loop(0, jnp.where(late == 0, 1, lanes), third_step, 0)

    for h in range(heads):
        landed(total_in, h, t_recv)
        settle(small_in.at[h], s_recv.at[h])
        vgrad_ref[0, h] = total[h] + decode(*refs_of(total_in, h))
        sums = small[(1 - late) * heads + h] + small_in[h]
        ggrad_ref[0, h : h + 1, :] = sums[0:1]
        ngrad_ref[0, h : h + 1, :] = sums[1:2]
        rgrad_ref[:, h : h + 1] = sums[2:3, 0:1]

    @pl.when(late == 1)
    def _():
        for h in range(heads):
            landed(i_in, h, i_recv)
            igrad_ref[0, h] = decode(*refs_of(i_in, h))

    settle(x_buf.at[:, pl.ds(0, chunks - 1)], x_send.at[0])
    settle(og_buf.at[:, pl.ds(0, chunks - 1)], og_send.at[0])
    settle(small_in, s_send.at[0])
    for part in range(2):
        settle(total_out[part], t_send.at[part])

    @pl.when(late == 0)
    def _():
        for part in range(2):
            settle(w_out[part], w_send.at[part])
            settle(i_in[part], g_send.at[part])

    @pl.when(late == 1)
    def _():
        for part in range(2):
            settle(g_out[part], g_send.at[part])

    settle(out_buf, out_send.at[0])
    settle(dx_buf, dx_send.at[0])
    settle(next_ref, out_recv.at[0])
    settle(prev_ref, dx_recv.at[0])


def hand_over(*refs):
    number = (len(refs) - 1) // 2
    order = sorted(range(number), key=lambda i: -refs[i].size)
    copies = [pltpu.make_async_copy(refs[i], refs[number + i], refs[-1].at[i]) for i in order]
    for copy in copies:
        copy.start()
    for copy in copies:
        copy.wait()


def per_device(segment_input, views, gate_vec, base_rate, norm_gain, init_weight, out_grad):
    count = lax.axis_size("ctx")
    size, features = segment_input.shape[1:]
    every, width = gate_vec.shape[1:]
    heads = every // count
    lanes, chunks = 2 * heads, count // 2

    def shaped(shape, kind):
        return jax.ShapeDtypeStruct(shape, kind)

    vmem = pl.BlockSpec(memory_space=pltpu.VMEM)
    hbm = pl.BlockSpec(memory_space=pltpu.HBM)

    def pairs(rows, columns):
        return pltpu.VMEM((lanes, chunks, 2, rows, columns), BF16)

    def floats(rows, columns):
        return pltpu.VMEM((lanes, chunks, rows, columns), F32)

    tokens = pltpu.VMEM((lanes, chunks, size, width), BF16)
    matrix = pltpu.VMEM((lanes, width, width), F32)
    semaphores = [
        (7,), (2,), (1,), (lanes,), (1,), (lanes,), (1,), (1,), (1,), (1,),
        (2,), (2, lanes), (2,), (2, lanes), (2, heads), (2,), (2, heads), (1,), (heads,),
    ]
    def coded(number, columns):
        return pltpu.VMEM((number, width, columns), BF16), pltpu.VMEM((number, 1, columns), F32)

    results = pl.pallas_call(
        functools.partial(kernel, count, lax.axis_size("segment"), heads, size, width),
        out_shape=(
            pltpu.VMEM((1, size, features), BF16),
            pltpu.VMEM((1, heads, width, 3 * width), F32),
            pltpu.VMEM((1, heads, width), F32),
            pltpu.VMEM((1, heads), F32),
            pltpu.VMEM((1, heads, width), F32),
            pltpu.VMEM((1, heads, width, width), F32),
            pltpu.VMEM((1, size, features), BF16),
        ),
        in_specs=[hbm] * 7,
        out_specs=(vmem,) * 7,
        scratch_shapes=[
            pltpu.VMEM(gate_vec.shape, F32),
            pltpu.VMEM(base_rate.shape, F32),
            pltpu.VMEM(norm_gain.shape, F32),
            pltpu.VMEM((lanes, width, 3 * width), BF16),
            tokens, tokens, tokens, tokens,
            pltpu.VMEM((3 + levels_of(size), size, size), F32),
            pairs(size, width), pairs(size, width), pairs(size, width), pairs(size, width), pairs(size, width),
            pairs(size, size), pairs(size, size), pairs(width, width),
            pairs(size, width), pairs(size, width), pairs(width, width), pairs(width, width),
            floats(size, width), floats(size, width), floats(size, width), floats(width, width),
            floats(size, width), floats(width, width), floats(size, width),
            floats(size, 1), floats(size, 1), floats(size, 1),
            matrix,
            *coded(lanes, width), *coded(lanes, width), *coded(lanes, width), *coded(lanes, width),
            *coded(heads, width),
            pltpu.VMEM((heads, width, 3 * width), F32),
            *coded(heads, 3 * width), *coded(heads, 3 * width),
            pltpu.VMEM((lanes, 8, width), F32),
            pltpu.VMEM((heads, 8, width), F32),
            *[pltpu.SemaphoreType.DMA(numbers) for numbers in semaphores],
        ],
        compiler_params=pltpu.CompilerParams(
            vmem_limit_bytes=52 * 1024 * 1024, collective_id=0, has_side_effects=True
        ),
    )(*[
        pltpu.with_memory_space_constraint(value, pltpu.HBM)
        for value in (segment_input, out_grad, views, gate_vec, base_rate, norm_gain, init_weight)
    ])
    results = [pltpu.with_memory_space_constraint(value, pltpu.VMEM) for value in results]
    return pl.pallas_call(
        hand_over,
        out_shape=tuple(shaped(value.shape, value.dtype) for value in results),
        in_specs=[vmem] * len(results),
        out_specs=(hbm,) * len(results),
        scratch_shapes=[pltpu.SemaphoreType.DMA((len(results),))],
    )(*results)


def solution(mesh):
    return jax.shard_map(
        per_device,
        mesh=mesh,
        in_specs=(
            P("segment", "ctx", None),
            P("segment", None, None, None),
            P("segment", None, None),
            P("segment", None),
            P("segment", None, None),
            P("segment", None, None, None),
            P("segment", "ctx", None),
        ),
        out_specs=(
            P("segment", "ctx", None),
            P("segment", "ctx", None, None),
            P("segment", "ctx", None),
            P("segment", "ctx"),
            P("segment", "ctx", None),
            P("segment", "ctx", None, None),
            P("segment", "ctx", None),
        ),
        check_vma=False,
    )
```
